512 devices in a mesh: rep: 8 (over x, core), fsdp: 8 (over z), tp: 8 (over y).
Axes of the slice: x: 4, y: 8, z: 8, core: 2. Of those that a mesh axis runs over, the one named last changes fastest.
Arguments:
- inputs: bfloat16 [1024, 4096], P('rep', 'tp'), may hold values from -6 to 6
- out_grads: bfloat16 [1024, 14336], P('rep', 'fsdp'), may hold values from -0.5 to 0.5
- error: bfloat16 [8, 4096, 14336], P('rep', 'tp', 'fsdp'), may hold values from -20 to 20
- q_init: bfloat16 [14336, 64], P('fsdp'), may hold values from -6 to 6
Outputs:
- new_error: bfloat16 [8, 4096, 14336], P('rep', 'tp', 'fsdp')
- p_factor: bfloat16 [4096, 64], P('tp')
- q_factor: bfloat16 [14336, 64], P('fsdp')
The draws below stay inside these ranges and needn't reach their ends.
All inputs are finite; a program needn't handle non-finite values.
Results may differ from the reference program's by a relative error of at most 0.0014.
Values sent between devices are 32-bit elements; how exact they have to be, the bound alone decides.
No kernel may reach another device: no remote copies, remote signals or barrier semaphores. Data moves between devices by JAX's collectives and lax.ppermute only.
A program may use at most 64 MiB of HBM per device.

```python
import math
import jax
import jax.numpy as jnp
from jax import lax

D = 4096
FF = 14336
R = 64
ITERS = 2
TOK = 128
REPLICAS = 8


def draw_error(key, part):
    key_noise = jax.random.fold_in(key, 11)
    key_rows = jax.random.fold_in(key, 12)
    key_cols = jax.random.fold_in(key, 13)
    row_pos = jnp.arange(D, dtype=jnp.float32) / max(D - 1, 1)
    row_scale = 3.0 ** row_pos * jnp.exp(jax.random.uniform(key_rows, (D,), jnp.float32, -0.4, 0.4))
    col_scale = jnp.exp(jax.random.uniform(key_cols, (FF,), jnp.float32, -0.7, 0.7))
    noise_draw = jax.random.truncated_normal(key_noise, -4.0, 4.0, (REPLICAS, D, FF), jnp.float32)
    scaled = 0.5 * noise_draw * row_scale[None, :, None] * col_scale[None, None, :]
    return scaled.astype(jnp.bfloat16)


def level_of(rng, shape, split, low, high):
    level = 1.0
    for axis_at, blocks in split:
        draws = jax.random.uniform(jax.random.fold_in(jax.random.fold_in(rng, 6), axis_at), (blocks,), jnp.float32, low / len(split), high / len(split))
        level = level * jnp.repeat(jnp.exp(draws), shape[axis_at] // blocks).reshape((-1,) + (1,) * (len(shape) - 1 - axis_at))
    return level


def scatter_about(stream_key, shape, deviation, limit, pieces=(), held_as=jnp.bfloat16):
    factor_of = level_of(stream_key, shape, pieces, -0.22, 0.18) if pieces else 1.0
    entries = jax.random.normal(stream_key, shape, jnp.float32) * deviation * factor_of
    return jnp.minimum(jnp.maximum(entries, -limit), limit).astype(held_as)


def setup_inputs(seed: int = 0) -> dict:
    streams_of = jax.random.split(jax.random.key(seed), 5)
    return {
        "inputs": scatter_about(streams_of[0], (REPLICAS * TOK, D), 1.0, 6.0, ((0, 8), (1, 8))),
        "out_grads": scatter_about(streams_of[1], (REPLICAS * TOK, FF), TOK ** -0.5, 0.5, ((0, 8), (1, 8))),
        "error": draw_error(jax.random.fold_in(streams_of[4], 71), 0),
        "q_init": scatter_about(streams_of[3], (FF, R), 1.0, 6.0, ((0, 8),)),
    }


exact_mode = lax.Precision.HIGHEST

def right_solve(factor, matrix):
    return jax.scipy.linalg.solve_triangular(factor, matrix.T, lower=True).T

def reference(inputs, out_grads, error, q_init):
    inputs_split = inputs.reshape(REPLICAS, TOK, D)
    grads_split = out_grads.reshape(REPLICAS, TOK, FF)

    def one_grad(pair):
        return lax.dot_general(pair[0].astype(jnp.float32), pair[1].astype(jnp.float32), (((0,), (0,)), ((), ())), preferred_element_type=jnp.float32)

    def accumulate(total, triple):
        merged = one_grad((triple[0], triple[1])) + triple[2].astype(jnp.float32)
        return (total + merged, None)
    summed, _ = lax.scan(accumulate, jnp.zeros((D, FF), jnp.float32), (inputs_split, grads_split, error))
    mean_merged = summed / REPLICAS
    q_full = q_init.astype(jnp.float32)
    p_basis = jnp.zeros((D, R), jnp.float32)
    for iteration in range(ITERS):
        p_full = jnp.dot(mean_merged, q_full, precision=exact_mode)
        gram = jnp.dot(p_full.T, p_full, precision=exact_mode)
        factor = jnp.linalg.cholesky(gram)
        p_basis = right_solve(factor, p_full)
        q_full = jnp.dot(mean_merged.T, p_basis, precision=exact_mode)
    approximation = jnp.dot(p_basis, q_full.T, precision=exact_mode)

    def new_one(triple):
        merged = one_grad((triple[0], triple[1])) + triple[2].astype(jnp.float32)
        return (merged - approximation).astype(jnp.bfloat16)
    new_error = lax.map(new_one, (inputs_split, grads_split, error))
    p_factor = (p_basis * math.sqrt(D)).astype(jnp.bfloat16)
    return (new_error, p_factor, q_full.astype(jnp.bfloat16))
```

```python
import functools
import math

import jax
import jax.numpy as jnp
from jax import lax
from jax.experimental import pallas as pl
from jax.experimental.pallas import tpu as pltpu
from jax.sharding import Mesh
from jax.sharding import PartitionSpec as P

D = 4096
R = 64
LANES = 128
REPLICAS = 8
XCZ = ("x", "core", "z")
XY = ("x", "y")
GRAM_COPIES = 4

f32 = jnp.float32
bf16 = jnp.bfloat16
NN = (((1,), (0,)), ((), ()))
NT = (((1,), (1,)), ((), ()))
TN = (((0,), (0,)), ((), ()))


def mxu(a, b, dims):
    return lax.dot_general(a, b, dims, preferred_element_type=f32)


def exact(a, b, dims):
    return lax.dot_general(
        a, b, dims, precision=lax.Precision.HIGHEST, preferred_element_type=f32
    )


def pieces(x):
    high = x.astype(bf16)
    return high, (x - high.astype(f32)).astype(bf16)


def stacked(x):
    return jnp.concatenate(pieces(x), axis=0)


def folded(x):
    return x[:R] + x[R:]


def call(kernel, name, out_shape, **kw):
    params = pltpu.CompilerParams(vmem_limit_bytes=kw.pop("vmem", 24 << 20))
    return pl.pallas_call(
        kernel, out_shape=out_shape, compiler_params=params, name=name, **kw
    )


def shape(s, dtype=f32):
    return jax.ShapeDtypeStruct(s, dtype)


def merge_kernel(core_ref, x_ref, g_ref, e_ref, q_ref, mine_ref, other_ref, part_ref):
    merged = mxu(x_ref[...], g_ref[...], TN) + e_ref[0].astype(f32)
    half = merged.shape[1] // 2

    @pl.when(core_ref[0] == 0)
    def _():
        mine_ref[...] = merged[:, :half]
        other_ref[...] = merged[:, half:]

    @pl.when(core_ref[0] != 0)
    def _():
        mine_ref[...] = merged[:, half:]
        other_ref[...] = merged[:, :half]

    high, low = pieces(merged)
    q = q_ref[...]
    part = mxu(high, q, NN) + mxu(low, q, NN)
    part_ref[0] = part.T * (1.0 / REPLICAS)


def merge(core, inputs, out_grads, error, q_init):
    tokens, rows = inputs.shape
    cols = out_grads.shape[1]
    blocks = rows // LANES
    spec = pltpu.PrefetchScalarGridSpec(
        num_scalar_prefetch=1,
        grid=(blocks,),
        in_specs=[
            pl.BlockSpec((tokens, LANES), lambda i, c: (0, i)),
            pl.BlockSpec((tokens, cols), lambda i, c: (0, 0)),
            pl.BlockSpec((1, LANES, cols), lambda i, c: (0, i, 0)),
            pl.BlockSpec((cols, R), lambda i, c: (0, 0)),
        ],
        out_specs=[
            pl.BlockSpec((LANES, cols // 2), lambda i, c: (i, 0)),
            pl.BlockSpec((LANES, cols // 2), lambda i, c: (i, 0)),
            pl.BlockSpec((1, R, LANES), lambda i, c: (i, 0, 0)),
        ],
    )
    outs = (
        shape((rows, cols // 2)),
        shape((rows, cols // 2)),
        shape((blocks, R, LANES)),
    )
    return call(merge_kernel, "merge", outs, grid_spec=spec)(
        core, inputs, out_grads, error, q_init
    )


def spread_kernel(lines, x_ref, o_ref):
    total = jnp.sum(x_ref[...], axis=0)
    if lines < 8:
        total = total[:lines] + total[lines:]
        total = jnp.concatenate([total, total], axis=0)
    o_ref[...] = jnp.broadcast_to(total[None], o_ref.shape)


def all_sum(parts, axes):
    size = lax.axis_size(axes)
    lines = parts.shape[0] * parts.shape[1] // size
    blocks = parts.reshape(size, lines, LANES)
    arrived = lax.all_to_all(blocks, axes, 0, 0, tiled=True)
    tall = max(lines, 8)
    arrived = arrived.reshape(-1, tall, LANES)
    again = call(
        functools.partial(spread_kernel, lines), "spread", shape(arrived.shape)
    )(arrived)
    whole = lax.all_to_all(again.reshape(blocks.shape), axes, 0, 0, tiled=True)
    return whole.reshape(parts.shape)


def side_by_side(ref, count):
    return jnp.concatenate([ref[i] for i in range(count)], axis=1)


def store_right(left, high, low, out_ref):
    blocks = high.shape[1] // LANES
    left_pieces = stacked(left)
    right = folded(mxu(left_pieces, high, NN) + mxu(left_pieces, low, NN))
    right = right * (1.0 / REPLICAS)
    for i in range(blocks):
        out_ref[i] = right[:, i * LANES : (i + 1) * LANES]
    gram = exact(left, left, NT) * (1.0 / GRAM_COPIES)
    out_ref[blocks] = jnp.concatenate([gram, jnp.zeros_like(gram)], axis=1)


def first_right_kernel(left_ref, mine_ref, came_ref, out_ref, high_ref, low_ref):
    high, low = pieces(mine_ref[...] + came_ref[...])
    high_ref[...] = high
    low_ref[...] = low
    store_right(side_by_side(left_ref, left_ref.shape[0]), high, low, out_ref)


def first_right(left, mine, came):
    rows, cols = mine.shape
    outs = (
        shape((cols // LANES + 1, R, LANES)),
        shape((rows, cols), bf16),
        shape((rows, cols), bf16),
    )
    return call(first_right_kernel, "first_right", outs)(left, mine, came)


def left_kernel(right_ref, high_ref, low_ref, out_ref):
    blocks = right_ref.shape[0] - 1
    right = stacked(side_by_side(right_ref, blocks))
    left = mxu(right, high_ref[...], NT) + mxu(right, low_ref[...], NT)
    left = folded(left) * (1.0 / REPLICAS)
    for i in range(out_ref.shape[0]):
        out_ref[i] = left[:, i * LANES : (i + 1) * LANES]


def left_part(right, high, low):
    outs = shape((high.shape[0] // LANES, R, LANES))
    return call(left_kernel, "left_part", outs)(right, high, low)


def second_right_kernel(
    inverse_ref, raw_ref, high_ref, low_ref, out_ref, left_ref
):
    raw = side_by_side(raw_ref, raw_ref.shape[0])
    left = exact(inverse_ref[...], raw, NN)
    left_ref[...] = left
    store_right(left, high_ref[...], low_ref[...], out_ref)


def second_right(inverse, raw, high, low):
    rows, cols = high.shape
    outs = (shape((cols // LANES + 1, R, LANES)), shape((R, rows)))
    return call(second_right_kernel, "second_right", outs)(inverse, raw, high, low)


def lower_inverse(gram):
    row = lax.broadcasted_iota(jnp.int32, (R, R), 0)
    column = lax.broadcasted_iota(jnp.int32, (R, R), 1)
    work = jnp.concatenate([gram, (row == column).astype(f32)], axis=1)
    bands = [work[8 * i : 8 * i + 8] for i in range(R // 8)]
    below = lax.broadcasted_iota(jnp.int32, (8, 1), 0)
    scales = []
    for k in range(R):
        at, line = divmod(k, 8)
        pivot_row = bands[at][line : line + 1]
        pivot = pivot_row[:, k : k + 1]
        scales.append(lax.rsqrt(pivot))
        scaled = pivot_row * (1.0 / pivot)
        for i in range(at, R // 8):
            factor = bands[i][:, k : k + 1]
            if i == at:
                factor = jnp.where(below > line, factor, 0.0)
            bands[i] = bands[i] - factor * scaled
    out = []
    for i in range(R // 8):
        scale = jnp.concatenate(scales[8 * i : 8 * i + 8], axis=0)
        out.append(bands[i][:, R:] * scale)
    return jnp.concatenate(out, axis=0)


def inverse_kernel(right_ref, out_ref):
    out_ref[...] = lower_inverse(right_ref[0][:, :R])


def last_block(right):
    last = right.shape[0] - 1
    return pl.BlockSpec((1, R, LANES), lambda i: (last, 0, 0))


def inverse_of(right):
    return call(
        inverse_kernel,
        "inverse",
        shape((R, R)),
        grid=(1,),
        in_specs=[last_block(right)],
        out_specs=pl.BlockSpec((R, R), lambda i: (0, 0)),
    )(right)


def basis_kernel(right_ref, left_ref, inverse_ref, basis_ref, factor_ref):
    inverse = lower_inverse(right_ref[0][:, :R])
    inverse_ref[...] = inverse
    basis = exact(inverse, left_ref[...], NN).T
    factor_ref[...] = (basis * math.sqrt(D)).astype(bf16)
    high, low = pieces(basis)
    basis_ref[...] = jnp.concatenate([high, high, low, low], axis=1)


def basis_of(right, left):
    rows = left.shape[1]
    whole = lambda i: (0, 0)
    return call(
        basis_kernel,
        "basis",
        (shape((R, R)), shape((rows, 4 * R), bf16), shape((rows, R), bf16)),
        grid=(1,),
        in_specs=[last_block(right), pl.BlockSpec((R, rows), whole)],
        out_specs=[
            pl.BlockSpec((R, R), whole),
            pl.BlockSpec((rows, 4 * R), whole),
            pl.BlockSpec((rows, R), whole),
        ],
    )(right, left)


def error_kernel(
    core_ref, inverse_ref, own_ref, came_ref, basis_ref, x_ref, g_ref, e_ref,
    new_ref, factor_ref, held_ref,
):
    blocks = own_ref.shape[0] - 1

    @pl.when(pl.program_id(0) == 0)
    def _():
        first = core_ref[0] == 0
        for half in range(2):
            take_own = first if half == 0 else jnp.logical_not(first)
            raw = jnp.concatenate(
                [jnp.where(take_own, own_ref[i], came_ref[i]) for i in range(blocks)],
                axis=1,
            )
            right = exact(inverse_ref[...], raw, NN)
            width = right.shape[1]
            factor_ref[half * width : (half + 1) * width] = right.T.astype(bf16)
            high, low = pieces(right)
            held_ref[:, half * width : (half + 1) * width] = jnp.concatenate(
                [high, low, high, low], axis=0
            )

    merged = mxu(x_ref[...], g_ref[...], TN) + e_ref[0].astype(f32)
    approximation = mxu(basis_ref[...], held_ref[...], NN)
    new_ref[0] = (merged - approximation).astype(bf16)


def final(core, inverse, own, came, basis, inputs, out_grads, error):
    tokens, rows = inputs.shape
    cols = out_grads.shape[1]
    fixed2 = lambda i, c: (0, 0)
    fixed3 = lambda i, c: (0, 0, 0)
    spec = pltpu.PrefetchScalarGridSpec(
        num_scalar_prefetch=1,
        grid=(rows // LANES,),
        in_specs=[
            pl.BlockSpec((R, R), fixed2),
            pl.BlockSpec(own.shape, fixed3),
            pl.BlockSpec(came.shape, fixed3),
            pl.BlockSpec((LANES, 4 * R), lambda i, c: (i, 0)),
            pl.BlockSpec((tokens, LANES), lambda i, c: (0, i)),
            pl.BlockSpec((tokens, cols), fixed2),
            pl.BlockSpec((1, LANES, cols), lambda i, c: (0, i, 0)),
        ],
        out_specs=[
            pl.BlockSpec((1, LANES, cols), lambda i, c: (0, i, 0)),
            pl.BlockSpec((cols, R), fixed2),
        ],
        scratch_shapes=[pltpu.VMEM((4 * R, cols), bf16)],
    )
    outs = (shape(error.shape, bf16), shape((cols, R), bf16))
    return call(error_kernel, "final", outs, grid_spec=spec)(
        core, inverse, own, came, basis, inputs, out_grads, error
    )


def shards(inputs, out_grads, error, q_init):
    core = lax.axis_index("core").reshape(1)
    swap = [(0, 1), (1, 0)]
    mine, other, part = merge(core, inputs, out_grads, error, q_init)
    came = lax.ppermute(other, "core", swap)
    left = all_sum(part, XCZ)
    part, high, low = first_right(left, mine, came)
    right = all_sum(part, XY)
    inverse = inverse_of(right)
    raw = all_sum(left_part(right, high, low), XCZ)
    part, left = second_right(inverse, raw, high, low)
    own = all_sum(part, XY)
    came = lax.ppermute(own, "core", swap)
    inverse, basis, p_factor = basis_of(own, left)
    new_error, q_factor = final(
        core, inverse, own, came, basis, inputs, out_grads, error
    )
    return new_error, p_factor, q_factor


def solution(mesh):
    rep, fsdp, tp = mesh.devices.shape
    fine = Mesh(mesh.devices.reshape(rep // 2, 2, fsdp, tp), ("x", "core", "z", "y"))
    both = ("x", "core")
    in_specs = (P(both, "y"), P(both, "z"), P(both, "y", "z"), P("z", None))
    out_specs = (P(both, "y", "z"), P("y", None), P("z", None))
    return jax.shard_map(
        shards, mesh=fine, in_specs=in_specs, out_specs=out_specs, check_vma=False
    )
```

```python
import functools
import math

import jax
import jax.numpy as jnp
from jax import lax
from jax.experimental import pallas as pl
from jax.experimental.pallas import tpu as pltpu
from jax.sharding import Mesh
from jax.sharding import PartitionSpec as P

D = 4096
R = 64
LANES = 128
REPLICAS = 8
XCZ = ("x", "core", "z")
XY = ("x", "y")
GRAM_COPIES = 4

f32 = jnp.float32
bf16 = jnp.bfloat16
NN = (((1,), (0,)), ((), ()))
NT = (((1,), (1,)), ((), ()))
TN = (((0,), (0,)), ((), ()))


def mxu(a, b, dims):
    return lax.dot_general(a, b, dims, preferred_element_type=f32)


def exact(a, b, dims):
    return lax.dot_general(
        a, b, dims, precision=lax.Precision.HIGHEST, preferred_element_type=f32
    )


def pieces(x):
    high = x.astype(bf16)
    return high, (x - high.astype(f32)).astype(bf16)


def stacked(x):
    return jnp.concatenate(pieces(x), axis=0)


def folded(x):
    return x[:R] + x[R:]


def call(kernel, name, out_shape, **kw):
    params = pltpu.CompilerParams(vmem_limit_bytes=kw.pop("vmem", 12 << 20))
    return pl.pallas_call(
        kernel, out_shape=out_shape, compiler_params=params, name=name, **kw
    )


def streamed(x):
    return pltpu.with_memory_space_constraint(x, pltpu.HBM)


def shape(s, dtype=f32):
    return jax.ShapeDtypeStruct(s, dtype)


def merge_kernel(core_ref, x_ref, g_ref, e_ref, q_ref, mine_ref, other_ref, part_ref):
    merged = mxu(x_ref[...], g_ref[...], TN) + e_ref[0].astype(f32)
    half = merged.shape[1] // 2

    @pl.when(core_ref[0] == 0)
    def _():
        mine_ref[...] = merged[:, :half]
        other_ref[...] = merged[:, half:]

    @pl.when(core_ref[0] != 0)
    def _():
        mine_ref[...] = merged[:, half:]
        other_ref[...] = merged[:, :half]

    high, low = pieces(merged)
    q = q_ref[...]
    part = mxu(q, high, NT) + mxu(q, low, NT)
    part_ref[0] = part * (1.0 / REPLICAS)


def merge(core, inputs, out_grads, error, q_init):
    tokens, rows = inputs.shape
    cols = out_grads.shape[1]
    blocks = rows // LANES
    spec = pltpu.PrefetchScalarGridSpec(
        num_scalar_prefetch=1,
        grid=(blocks,),
        in_specs=[
            pl.BlockSpec((tokens, LANES), lambda i, c: (0, i)),
            pl.BlockSpec((tokens, cols), lambda i, c: (0, 0)),
            pl.BlockSpec((1, LANES, cols), lambda i, c: (0, i, 0)),
            pl.BlockSpec((R, cols), lambda i, c: (0, 0)),
        ],
        out_specs=[
            pl.BlockSpec((LANES, cols // 2), lambda i, c: (i, 0)),
            pl.BlockSpec((LANES, cols // 2), lambda i, c: (i, 0)),
            pl.BlockSpec((1, R, LANES), lambda i, c: (i, 0, 0)),
        ],
    )
    outs = (
        shape((rows, cols // 2)),
        shape((rows, cols // 2)),
        shape((blocks, R, LANES)),
    )
    return call(merge_kernel, "merge", outs, grid_spec=spec)(
        core, *(streamed(a) for a in (inputs, out_grads, error, q_init.T))
    )


def spread_kernel(lines, x_ref, o_ref):
    total = jnp.sum(x_ref[...], axis=0)
    if lines < 8:
        total = total[:lines] + total[lines:]
        total = jnp.concatenate([total, total], axis=0)
    o_ref[...] = jnp.broadcast_to(total[None], o_ref.shape)


def all_sum(parts, axes):
    size = lax.axis_size(axes)
    lines = parts.shape[0] * parts.shape[1] // size
    blocks = parts.reshape(size, lines, LANES)
    arrived = lax.all_to_all(blocks, axes, 0, 0, tiled=True)
    tall = max(lines, 8)
    arrived = arrived.reshape(-1, tall, LANES)
    again = call(
        functools.partial(spread_kernel, lines), "spread", shape(arrived.shape)
    )(arrived)
    whole = lax.all_to_all(again.reshape(blocks.shape), axes, 0, 0, tiled=True)
    return whole.reshape(parts.shape)


def ring_sum(parts):
    inner, outer = ("x", "core"), "z"
    lines = parts.shape[0] * parts.shape[1] // lax.axis_size(inner)

    def passed_on(blocks, axes):
        arrived = lax.all_to_all(blocks, axes, 0, 0, tiled=True)
        again = shape((lax.axis_size(outer if axes == inner else inner), lines, LANES))
        return call(functools.partial(spread_kernel, lines), "spread", again)(arrived)

    blocks = passed_on(parts.reshape(-1, lines, LANES), inner)
    blocks = passed_on(blocks, outer)
    whole = lax.all_to_all(blocks, inner, 0, 0, tiled=True)
    return whole.reshape(parts.shape)


def side_by_side(ref, count):
    return jnp.concatenate([ref[i] for i in range(count)], axis=1)


def store_right(left, high, low, out_ref):
    blocks = high.shape[1] // LANES
    left_pieces = stacked(left)
    right = folded(mxu(left_pieces, high, NN) + mxu(left_pieces, low, NN))
    right = right * (1.0 / REPLICAS)
    for i in range(blocks):
        out_ref[i] = right[:, i * LANES : (i + 1) * LANES]
    gram = exact(left, left, NT) * (1.0 / GRAM_COPIES)
    out_ref[blocks] = jnp.concatenate([gram, jnp.zeros_like(gram)], axis=1)


def first_right_kernel(left_ref, mine_ref, came_ref, out_ref, high_ref, low_ref):
    high, low = pieces(mine_ref[...] + came_ref[...])
    high_ref[...] = high
    low_ref[...] = low
    store_right(side_by_side(left_ref, left_ref.shape[0]), high, low, out_ref)


def first_right(left, mine, came):
    rows, cols = mine.shape
    outs = (
        shape((cols // LANES + 1, R, LANES)),
        shape((rows, cols), bf16),
        shape((rows, cols), bf16),
    )
    return call(first_right_kernel, "first_right", outs)(left, mine, came)


def left_kernel(right_ref, high_ref, low_ref, out_ref):
    blocks = right_ref.shape[0] - 1
    right = stacked(side_by_side(right_ref, blocks))
    left = mxu(right, high_ref[...], NT) + mxu(right, low_ref[...], NT)
    left = folded(left) * (1.0 / REPLICAS)
    for i in range(out_ref.shape[0]):
        out_ref[i] = left[:, i * LANES : (i + 1) * LANES]


def left_part(right, high, low):
    outs = shape((high.shape[0] // LANES, R, LANES))
    return call(left_kernel, "left_part", outs)(right, high, low)


def second_right_kernel(
    inverse_ref, raw_ref, high_ref, low_ref, out_ref, left_ref
):
    raw = side_by_side(raw_ref, raw_ref.shape[0])
    left = exact(inverse_ref[...], raw, NN)
    left_ref[...] = left
    store_right(left, high_ref[...], low_ref[...], out_ref)


def second_right(inverse, raw, high, low):
    rows, cols = high.shape
    outs = (shape((cols // LANES + 1, R, LANES)), shape((R, rows)))
    return call(second_right_kernel, "second_right", outs)(inverse, raw, high, low)


def lower_inverse(gram):
    row = lax.broadcasted_iota(jnp.int32, (R, R), 0)
    column = lax.broadcasted_iota(jnp.int32, (R, R), 1)
    work = jnp.concatenate([gram, (row == column).astype(f32)], axis=1)
    bands = [work[8 * i : 8 * i + 8] for i in range(R // 8)]
    below = lax.broadcasted_iota(jnp.int32, (8, LANES), 0)
    scales = []
    for p in range(R // 8):
        live = range(p, R // 8)
        spread = {
            i: [
                jnp.broadcast_to(bands[i][:, 8 * p + c : 8 * p + c + 1], (8, LANES))
                for c in range(8)
            ]
            for i in live
        }
        for k in range(8):
            pivot_row = bands[p][k : k + 1]
            pivots = [spread[p][c][k : k + 1] for c in range(8)]
            scales.append(lax.rsqrt(pivots[k]))
            inverse = 1.0 / pivots[k]
            for i in live:
                factor = spread[i][k] * inverse
                if i == p:
                    factor = jnp.where(below > k, factor, 0.0)
                for c in range(k + 1, 8):
                    spread[i][c] = spread[i][c] - factor * pivots[c]
                bands[i] = bands[i] - factor * pivot_row
    out = []
    for i in range(R // 8):
        scale = jnp.concatenate(scales[8 * i : 8 * i + 8], axis=0)
        out.append(bands[i][:, R:] * scale[:, R:])
    return jnp.concatenate(out, axis=0)


def inverse_kernel(right_ref, out_ref):
    out_ref[...] = lower_inverse(right_ref[0][:, :R])


def last_block(right):
    last = right.shape[0] - 1
    return pl.BlockSpec((1, R, LANES), lambda i: (last, 0, 0))


def inverse_of(right):
    return call(
        inverse_kernel,
        "inverse",
        shape((R, R)),
        grid=(1,),
        in_specs=[last_block(right)],
        out_specs=pl.BlockSpec((R, R), lambda i: (0, 0)),
    )(right)


def basis_kernel(right_ref, left_ref, inverse_ref, basis_ref, factor_ref):
    inverse = lower_inverse(right_ref[0][:, :R])
    inverse_ref[...] = inverse
    basis = exact(inverse, left_ref[...], NN)
    factor_ref[...] = (basis * math.sqrt(D)).astype(bf16)
    high, low = pieces(basis.T)
    basis_ref[...] = jnp.concatenate([high, high, low, low], axis=1)


def basis_of(right, left):
    rows = left.shape[1]
    whole = lambda i: (0, 0)
    return call(
        basis_kernel,
        "basis",
        (shape((R, R)), shape((rows, 4 * R), bf16), shape((R, rows), bf16)),
        grid=(1,),
        in_specs=[last_block(right), pl.BlockSpec((R, rows), whole)],
        out_specs=[
            pl.BlockSpec((R, R), whole),
            pl.BlockSpec((rows, 4 * R), whole),
            pl.BlockSpec((R, rows), whole),
        ],
    )(right, left)


def error_kernel(
    core_ref, inverse_ref, own_ref, came_ref, basis_ref, x_ref, g_ref, e_ref,
    new_ref, factor_ref, held_ref,
):
    blocks = own_ref.shape[0] - 1

    @pl.when(pl.program_id(0) == 0)
    def _():
        first = core_ref[0] == 0
        for half in range(2):
            take_own = first if half == 0 else jnp.logical_not(first)
            raw = jnp.concatenate(
                [jnp.where(take_own, own_ref[i], came_ref[i]) for i in range(blocks)],
                axis=1,
            )
            right = exact(inverse_ref[...], raw, NN)
            width = right.shape[1]
            factor_ref[:, half * width : (half + 1) * width] = right.astype(bf16)
            high, low = pieces(right)
            held_ref[:, half * width : (half + 1) * width] = jnp.concatenate(
                [high, low, high, low], axis=0
            )

    merged = mxu(x_ref[...], g_ref[...], TN) + e_ref[0].astype(f32)
    approximation = mxu(basis_ref[...], held_ref[...], NN)
    new_ref[0] = (merged - approximation).astype(bf16)


def final(core, inverse, own, came, basis, inputs, out_grads, error):
    tokens, rows = inputs.shape
    cols = out_grads.shape[1]
    fixed2 = lambda i, c: (0, 0)
    fixed3 = lambda i, c: (0, 0, 0)
    spec = pltpu.PrefetchScalarGridSpec(
        num_scalar_prefetch=1,
        grid=(rows // LANES,),
        in_specs=[
            pl.BlockSpec((R, R), fixed2),
            pl.BlockSpec(own.shape, fixed3),
            pl.BlockSpec(came.shape, fixed3),
            pl.BlockSpec((LANES, 4 * R), lambda i, c: (i, 0)),
            pl.BlockSpec((tokens, LANES), lambda i, c: (0, i)),
            pl.BlockSpec((tokens, cols), fixed2),
            pl.BlockSpec((1, LANES, cols), lambda i, c: (0, i, 0)),
        ],
        out_specs=[
            pl.BlockSpec((1, LANES, cols), lambda i, c: (0, i, 0)),
            pl.BlockSpec((R, cols), fixed2),
        ],
        scratch_shapes=[pltpu.VMEM((4 * R, cols), bf16)],
    )
    outs = (shape(error.shape, bf16), shape((R, cols), bf16))
    return call(error_kernel, "final", outs, grid_spec=spec)(
        core, inverse, own, came, basis, inputs, out_grads, error
    )


def shards(inputs, out_grads, error, q_init):
    core = lax.axis_index("core").reshape(1)
    swap = [(0, 1), (1, 0)]
    mine, other, part = merge(core, inputs, out_grads, error, q_init)
    came = lax.ppermute(other, "core", swap)
    left = ring_sum(part)
    part, high, low = first_right(left, mine, came)
    right = all_sum(part, XY)
    inverse = inverse_of(right)
    raw = ring_sum(left_part(right, high, low))
    part, left = second_right(inverse, raw, high, low)
    own = all_sum(part, XY)
    came = lax.ppermute(own, "core", swap)
    inverse, basis, p_factor = basis_of(own, left)
    new_error, q_factor = final(
        core, inverse, own, came, basis, inputs, out_grads, error
    )
    return new_error, p_factor.T, q_factor.T


def solution(mesh):
    rep, fsdp, tp = mesh.devices.shape
    fine = Mesh(mesh.devices.reshape(rep // 2, 2, fsdp, tp), ("x", "core", "z", "y"))
    both = ("x", "core")
    in_specs = (P(both, "y"), P(both, "z"), P(both, "y", "z"), P("z", None))
    out_specs = (P(both, "y", "z"), P("y", None), P("z", None))
    return jax.shard_map(
        shards, mesh=fine, in_specs=in_specs, out_specs=out_specs, check_vma=False
    )
```

```python
import math

import jax
import jax.numpy as jnp
from jax import lax
from jax.experimental import pallas as pl
from jax.experimental.pallas import tpu as pltpu
from jax.sharding import Mesh
from jax.sharding import PartitionSpec as P

D = 4096
R = 64
LANES = 128
TALL = 256
REPLICAS = 8
XC = ("x", "core")
XY = ("x", "y")
GRAM_COPIES = 4

f32 = jnp.float32
bf16 = jnp.bfloat16
NN = (((1,), (0,)), ((), ()))
NT = (((1,), (1,)), ((), ()))
TN = (((0,), (0,)), ((), ()))


def mxu(a, b, dims):
    return lax.dot_general(a, b, dims, preferred_element_type=f32)


def exact(a, b, dims):
    return lax.dot_general(
        a, b, dims, precision=lax.Precision.HIGHEST, preferred_element_type=f32
    )


def pieces(x):
    high = x.astype(bf16)
    return high, (x - high.astype(f32)).astype(bf16)


def stacked(x):
    return jnp.concatenate(pieces(x), axis=0)


def folded(x):
    return x[:R] + x[R:]


def across(a):
    high, low = pieces(a)
    return jnp.concatenate([high, high, low, low], axis=1)


def down(b):
    high, low = pieces(b)
    return jnp.concatenate([high, low, high, low], axis=0)


def call(kernel, out_shape, **kw):
    params = pltpu.CompilerParams(vmem_limit_bytes=kw.pop("vmem", 12 << 20))
    return pl.pallas_call(kernel, out_shape=out_shape, compiler_params=params, **kw)


def streamed(x):
    return pltpu.with_memory_space_constraint(x, pltpu.HBM)


def shape(s, dtype=f32):
    return jax.ShapeDtypeStruct(s, dtype)


def times_q(a, q_ref):
    half = a.shape[1] // 2
    parts = [
        mxu(a[:, part], q_ref[:, part], NT) for part in (slice(half), slice(half, None))
    ]
    return (parts[0] + parts[1]).T


def first_left_kernel(
    x_hbm, g_hbm, e_hbm, q_hbm, part_ref, x_ref, g_ref, e_ref, q_ref, here
):
    rows = e_ref.shape[0]
    pairs = [(q_hbm, q_ref), (g_hbm, g_ref), (x_hbm, x_ref)]
    for at in range(0, rows, TALL):
        lines = pl.ds(at, TALL)
        pairs.append((e_hbm.at[0, lines], e_ref.at[lines]))
    copies = [
        pltpu.make_async_copy(source, target, here.at[i])
        for i, (source, target) in enumerate(pairs)
    ]
    for copy in copies:
        copy.start()
    copies[0].wait()
    copies[1].wait()
    through = stacked(times_q(g_ref[...], q_ref))
    copies[2].wait()
    left = folded(mxu(through, x_ref[...], NN))
    for i, at in enumerate(range(0, rows, TALL)):
        lines = slice(at, at + TALL)
        copies[3 + i].wait()
        part = (times_q(e_ref[lines], q_ref) + left[:, lines]) * (1.0 / REPLICAS)
        for j in range(TALL // LANES):
            block = part[:, j * LANES : (j + 1) * LANES]
            part_ref[at // LANES + j] = block


def first_left(inputs, out_grads, error, q_init):
    rows = inputs.shape[1]
    operands = (inputs, out_grads, error, q_init.T)
    held = [pltpu.VMEM(a.shape[-2:], bf16) for a in operands]
    return call(
        first_left_kernel,
        shape((rows // LANES, R, LANES)),
        in_specs=[pl.BlockSpec(memory_space=pltpu.HBM)] * 4,
        out_specs=pl.BlockSpec(memory_space=pltpu.VMEM),
        scratch_shapes=held + [pltpu.SemaphoreType.DMA((3 + rows // TALL,))],
    )(*(streamed(a) for a in operands))


def merge_kernel(core_ref, x_ref, g_ref, e_ref, mine_ref, other_ref):
    merged = mxu(x_ref[...], g_ref[...], TN) + e_ref[0].astype(f32)
    half = merged.shape[1] // 2

    @pl.when(core_ref[0] == 0)
    def _():
        mine_ref[...] = merged[:, :half]
        other_ref[...] = merged[:, half:]

    @pl.when(core_ref[0] != 0)
    def _():
        mine_ref[...] = merged[:, half:]
        other_ref[...] = merged[:, :half]


def merge(core, inputs, out_grads, error):
    tokens, rows = inputs.shape
    cols = out_grads.shape[1]
    half = pl.BlockSpec((TALL, cols // 2), lambda i, c: (i, 0))
    spec = pltpu.PrefetchScalarGridSpec(
        num_scalar_prefetch=1,
        grid=(rows // TALL,),
        in_specs=[
            pl.BlockSpec((tokens, TALL), lambda i, c: (0, i)),
            pl.BlockSpec((tokens, cols), lambda i, c: (0, 0)),
            pl.BlockSpec((1, TALL, cols), lambda i, c: (0, i, 0)),
        ],
        out_specs=[half, half],
    )
    outs = (pltpu.HBM((rows, cols // 2), f32), pltpu.HBM((rows, cols // 2), f32))
    cost = pl.CostEstimate(
        flops=2 * tokens * rows * cols, bytes_accessed=12 * rows * cols, transcendentals=0
    )
    return call(merge_kernel, outs, grid_spec=spec, cost_estimate=cost)(
        core, *(streamed(a) for a in (inputs, out_grads, error))
    )


def spread_kernel(x_ref, o_ref):
    total = jnp.sum(x_ref[...], axis=0)
    o_ref[...] = jnp.broadcast_to(total[None], o_ref.shape)


def sent(blocks, axes):
    return lax.all_to_all(blocks, axes, 0, 0, tiled=True)


def spread(arrived, count):
    again = shape((count, *arrived.shape[1:]))
    return call(spread_kernel, again)(arrived)


def all_sum(parts, axes):
    size = lax.axis_size(axes)
    lines = parts.shape[0] * parts.shape[1] // size
    arrived = sent(parts.reshape(size, lines, LANES), axes)
    return sent(spread(arrived, size), axes).reshape(parts.shape)


def ring_sum(parts, outer, inner):
    count = lax.axis_size(outer)
    lines = parts.shape[0] * parts.shape[1] // count
    arrived = sent(parts.reshape(count, lines, LANES), outer)
    arrived = sent(spread(arrived, lax.axis_size(inner)), inner)
    return sent(spread(arrived, count), outer).reshape(parts.shape)


def side_by_side(ref, count):
    return jnp.concatenate([ref[i] for i in range(count)], axis=1)


def store_right(left, high, low, out_ref):
    blocks = high.shape[1] // LANES
    left_pieces = stacked(left)
    right = folded(mxu(left_pieces, high, NN) + mxu(left_pieces, low, NN))
    right = right * (1.0 / REPLICAS)
    for i in range(blocks):
        out_ref[i] = right[:, i * LANES : (i + 1) * LANES]
    gram = exact(left, left, NT) * (1.0 / GRAM_COPIES)
    out_ref[blocks] = jnp.concatenate([gram, jnp.zeros_like(gram)], axis=1)


def halve_kernel(mine_ref, came_ref, high_ref, low_ref):
    high_ref[...], low_ref[...] = pieces(mine_ref[...] + came_ref[...])


def halve(mine, came):
    outs = (shape(mine.shape, bf16), shape(mine.shape, bf16))
    cost = pl.CostEstimate(
        flops=3 * mine.size, bytes_accessed=12 * mine.size, transcendentals=0
    )
    block = pl.BlockSpec((TALL, mine.shape[1]), lambda i: (i, 0))
    return call(
        halve_kernel,
        outs,
        grid=(mine.shape[0] // TALL,),
        in_specs=[block, block],
        out_specs=[block, block],
        cost_estimate=cost,
    )(streamed(mine), streamed(came))


def first_right_kernel(left_ref, high_ref, low_ref, out_ref):
    left = side_by_side(left_ref, left_ref.shape[0])
    store_right(left, high_ref[...], low_ref[...], out_ref)


def first_right(left, high, low):
    outs = shape((high.shape[1] // LANES + 1, R, LANES))
    return call(first_right_kernel, outs)(left, high, low)


def left_kernel(right_ref, high_ref, low_ref, out_ref):
    blocks = right_ref.shape[0] - 1
    right = stacked(side_by_side(right_ref, blocks))
    left = mxu(right, high_ref[...], NT) + mxu(right, low_ref[...], NT)
    left = folded(left) * (1.0 / REPLICAS)
    for i in range(out_ref.shape[0]):
        out_ref[i] = left[:, i * LANES : (i + 1) * LANES]


def left_part(right, high, low):
    outs = shape((high.shape[0] // LANES, R, LANES))
    return call(left_kernel, outs)(right, high, low)


def second_right_kernel(
    inverse_ref, raw_ref, high_ref, low_ref, out_ref, left_ref
):
    raw = side_by_side(raw_ref, raw_ref.shape[0])
    left = exact(inverse_ref[...], raw, NN)
    left_ref[...] = left
    store_right(left, high_ref[...], low_ref[...], out_ref)


def second_right(inverse, raw, high, low):
    rows, cols = high.shape
    outs = (shape((cols // LANES + 1, R, LANES)), shape((R, rows)))
    return call(second_right_kernel, outs)(inverse, raw, high, low)


def lower_inverse(gram):
    row = lax.broadcasted_iota(jnp.int32, (R, R), 0)
    column = lax.broadcasted_iota(jnp.int32, (R, R), 1)
    work = jnp.concatenate([gram, (row == column).astype(f32)], axis=1)
    bands = [work[8 * i : 8 * i + 8] for i in range(R // 8)]
    below = lax.broadcasted_iota(jnp.int32, (8, LANES), 0)
    scales = []
    for p in range(R // 8):
        live = range(p, R // 8)
        spread = {
            i: [
                jnp.broadcast_to(bands[i][:, 8 * p + c : 8 * p + c + 1], (8, LANES))
                for c in range(8)
            ]
            for i in live
        }
        for k in range(8):
            pivot_row = bands[p][k : k + 1]
            pivots = [spread[p][c][k : k + 1] for c in range(8)]
            scales.append(lax.rsqrt(pivots[k]))
            inverse = 1.0 / pivots[k]
            for i in live:
                factor = spread[i][k] * inverse
                if i == p:
                    factor = jnp.where(below > k, factor, 0.0)
                for c in range(k + 1, 8):
                    spread[i][c] = spread[i][c] - factor * pivots[c]
                bands[i] = bands[i] - factor * pivot_row
    out = []
    for i in range(R // 8):
        scale = jnp.concatenate(scales[8 * i : 8 * i + 8], axis=0)
        out.append(bands[i][:, R:] * scale[:, R:])
    return jnp.concatenate(out, axis=0)


def inverse_kernel(right_ref, out_ref):
    out_ref[...] = lower_inverse(right_ref[0][:, :R])


def last_block(right):
    last = right.shape[0] - 1
    return pl.BlockSpec((1, R, LANES), lambda i: (last, 0, 0))


def inverse_of(right):
    return call(
        inverse_kernel,
        shape((R, R)),
        grid=(1,),
        in_specs=[last_block(right)],
        out_specs=pl.BlockSpec((R, R), lambda i: (0, 0)),
    )(right)


def basis_kernel(right_ref, left_ref, inverse_ref, basis_ref, factor_ref):
    inverse = lower_inverse(right_ref[0][:, :R])
    inverse_ref[...] = inverse
    basis = exact(inverse, left_ref[...], NN)
    factor_ref[...] = (basis * math.sqrt(D)).astype(bf16)
    basis_ref[...] = across(basis.T)


def basis_of(right, left):
    rows = left.shape[1]
    whole = lambda i: (0, 0)
    return call(
        basis_kernel,
        (shape((R, R)), shape((rows, 4 * R), bf16), shape((R, rows), bf16)),
        grid=(1,),
        in_specs=[last_block(right), pl.BlockSpec((R, rows), whole)],
        out_specs=[
            pl.BlockSpec((R, R), whole),
            pl.BlockSpec((rows, 4 * R), whole),
            pl.BlockSpec((R, rows), whole),
        ],
    )(right, left)


def error_kernel(
    core_ref, inverse_ref, own_ref, came_ref, basis_ref, x_ref, g_ref, e_ref,
    new_ref, factor_ref, held_ref, done_ref, sent_sem,
):
    width = g_ref.shape[1] // 2
    inverse = across(inverse_ref[...])
    for half, raw_ref in enumerate((own_ref, came_ref)):
        start = lax.rem(core_ref[0] + half, 2) * width
        columns = pl.ds(pl.multiple_of(start, LANES), width)
        raw = side_by_side(raw_ref, raw_ref.shape[0] - 1)
        right = mxu(inverse, down(raw), NN)
        factor_ref[:, columns] = right.astype(bf16)
        held_ref[:, columns] = down(right)
    count, _, step = done_ref.shape
    turned = x_ref[...].T
    copies = []
    for i in range(count):
        columns = pl.ds(i * step, step)
        merged = mxu(turned, g_ref[:, columns], NN) + e_ref[0, :, columns].astype(f32)
        approximation = mxu(basis_ref[...], held_ref[:, columns], NN)
        done_ref[i] = (merged - approximation).astype(bf16)
        copies.append(
            pltpu.make_async_copy(
                done_ref.at[i], new_ref.at[0, :, columns], sent_sem.at[i]
            )
        )
        copies[-1].start()
    for copy in copies:
        copy.wait()


def final(core, inverse, own, came, basis, inputs, out_grads, error):
    rows = inputs.shape[1]
    cols = out_grads.shape[1]
    step = 2 * LANES
    count = cols // step
    vmem = pl.BlockSpec(memory_space=pltpu.VMEM)
    outs = (shape(error.shape, bf16), shape((R, cols), bf16))
    return call(
        error_kernel,
        outs,
        in_specs=[pl.BlockSpec(memory_space=pltpu.SMEM)] + [vmem] * 7,
        out_specs=[pl.BlockSpec(memory_space=pltpu.HBM), vmem],
        scratch_shapes=[
            pltpu.VMEM((4 * R, cols), bf16),
            pltpu.VMEM((count, rows, step), bf16),
            pltpu.SemaphoreType.DMA((count,)),
        ],
    )(core, inverse, own, came, basis, inputs, out_grads, error)


def shards(inputs, out_grads, error, q_init):
    core = lax.axis_index("core").reshape(1)
    swap = [(0, 1), (1, 0)]
    part = first_left(inputs, out_grads, error, q_init)
    mine, other = merge(core, inputs, out_grads, error)
    came = lax.ppermute(other, "core", swap)
    left = ring_sum(part, XC, "z")
    high, low = halve(mine, came)
    right = all_sum(first_right(left, high, low), XY)
    inverse = inverse_of(right)
    raw = ring_sum(left_part(right, high, low), XC, "z")
    part, left = second_right(inverse, raw, high, low)
    own = all_sum(part, XY)
    came = lax.ppermute(own, "core", swap)
    inverse, basis, p_factor = basis_of(own, left)
    new_error, q_factor = final(
        core, inverse, own, came, basis, inputs, out_grads, error
    )
    return new_error, p_factor.T, q_factor.T


def solution(mesh):
    rep, fsdp, tp = mesh.devices.shape
    fine = Mesh(mesh.devices.reshape(rep // 2, 2, fsdp, tp), ("x", "core", "z", "y"))
    both = ("x", "core")
    in_specs = (P(both, "y"), P(both, "z"), P(both, "y", "z"), P("z", None))
    out_specs = (P(both, "y", "z"), P("y", None), P("z", None))
    return jax.shard_map(
        shards, mesh=fine, in_specs=in_specs, out_specs=out_specs, check_vma=False
    )
```

```python
import math

import jax
import jax.numpy as jnp
from jax import lax
from jax.experimental import pallas as pl
from jax.experimental.pallas import tpu as pltpu
from jax.sharding import Mesh
from jax.sharding import PartitionSpec as P

D = 4096
R = 64
LANES = 128
TALL = 256
REPLICAS = 8
XC = ("x", "core")
XY = ("x", "y")
GRAM_COPIES = 4

f32 = jnp.float32
bf16 = jnp.bfloat16
NN = (((1,), (0,)), ((), ()))
NT = (((1,), (1,)), ((), ()))
TN = (((0,), (0,)), ((), ()))


def mxu(a, b, dims):
    return lax.dot_general(a, b, dims, preferred_element_type=f32)


def exact(a, b, dims):
    return lax.dot_general(
        a, b, dims, precision=lax.Precision.HIGHEST, preferred_element_type=f32
    )


def pieces(x):
    high = x.astype(bf16)
    return high, (x - high.astype(f32)).astype(bf16)


def stacked(x):
    return jnp.concatenate(pieces(x), axis=0)


def folded(x):
    return x[:R] + x[R:]


def across(a):
    high, low = pieces(a)
    return jnp.concatenate([high, high, low, low], axis=1)


def down(b):
    high, low = pieces(b)
    return jnp.concatenate([high, low, high, low], axis=0)


def call(kernel, out_shape, **kw):
    params = pltpu.CompilerParams(vmem_limit_bytes=kw.pop("vmem", 12 << 20))
    return pl.pallas_call(kernel, out_shape=out_shape, compiler_params=params, **kw)


def streamed(x):
    return pltpu.with_memory_space_constraint(x, pltpu.HBM)


def shape(s, dtype=f32):
    return jax.ShapeDtypeStruct(s, dtype)


def shrinking(rows):
    blocks = [(at, TALL) for at in range(0, rows - TALL, TALL)]
    return blocks + [(at, LANES) for at in range(rows - TALL, rows, LANES)]


def times_q(a, q_ref):
    half = a.shape[1] // 2
    parts = [
        mxu(a[:, part], q_ref[:, part], NT) for part in (slice(half), slice(half, None))
    ]
    return (parts[0] + parts[1]).T


def first_left_kernel(
    x_hbm, g_hbm, e_hbm, q_hbm, part_ref, x_ref, g_ref, e_ref, q_ref, here
):
    rows = e_ref.shape[0]
    pairs = [(q_hbm, q_ref), (g_hbm, g_ref), (x_hbm, x_ref)]
    for at, height in shrinking(rows):
        lines = pl.ds(at, height)
        pairs.append((e_hbm.at[0, lines], e_ref.at[lines]))
    copies = [
        pltpu.make_async_copy(source, target, here.at[i])
        for i, (source, target) in enumerate(pairs)
    ]
    for copy in copies:
        copy.start()
    copies[0].wait()
    copies[1].wait()
    through = stacked(times_q(g_ref[...], q_ref))
    copies[2].wait()
    left = folded(mxu(through, x_ref[...], NN))
    for i, (at, height) in enumerate(shrinking(rows)):
        lines = slice(at, at + height)
        copies[3 + i].wait()
        part = (times_q(e_ref[lines], q_ref) + left[:, lines]) * (1.0 / REPLICAS)
        for j in range(height // LANES):
            block = part[:, j * LANES : (j + 1) * LANES]
            part_ref[at // LANES + j] = block


def first_left(inputs, out_grads, error, q_init):
    rows = inputs.shape[1]
    operands = (inputs, out_grads, error, q_init.T)
    held = [pltpu.VMEM(a.shape[-2:], bf16) for a in operands]
    return call(
        first_left_kernel,
        shape((rows // LANES, R, LANES)),
        in_specs=[pl.BlockSpec(memory_space=pltpu.HBM)] * 4,
        out_specs=pl.BlockSpec(memory_space=pltpu.VMEM),
        scratch_shapes=held + [pltpu.SemaphoreType.DMA((3 + len(shrinking(rows)),))],
    )(*(streamed(a) for a in operands))


def merge_kernel(core_ref, x_ref, g_ref, e_ref, mine_ref, other_ref):
    merged = mxu(x_ref[...], g_ref[...], TN) + e_ref[0].astype(f32)
    half = merged.shape[1] // 2

    @pl.when(core_ref[0] == 0)
    def _():
        mine_ref[...] = merged[:, :half]
        other_ref[...] = merged[:, half:]

    @pl.when(core_ref[0] != 0)
    def _():
        mine_ref[...] = merged[:, half:]
        other_ref[...] = merged[:, :half]


def merge(core, inputs, out_grads, error):
    tokens, rows = inputs.shape
    cols = out_grads.shape[1]
    half = pl.BlockSpec((TALL, cols // 2), lambda i, c: (i, 0))
    spec = pltpu.PrefetchScalarGridSpec(
        num_scalar_prefetch=1,
        grid=(rows // TALL,),
        in_specs=[
            pl.BlockSpec((tokens, TALL), lambda i, c: (0, i)),
            pl.BlockSpec((tokens, cols), lambda i, c: (0, 0)),
            pl.BlockSpec((1, TALL, cols), lambda i, c: (0, i, 0)),
        ],
        out_specs=[half, half],
    )
    outs = (pltpu.HBM((rows, cols // 2), f32), pltpu.HBM((rows, cols // 2), f32))
    cost = pl.CostEstimate(
        flops=2 * tokens * rows * cols, bytes_accessed=12 * rows * cols, transcendentals=0
    )
    return call(merge_kernel, outs, grid_spec=spec, cost_estimate=cost)(
        core, *(streamed(a) for a in (inputs, out_grads, error))
    )


def spread_kernel(x_ref, o_ref):
    total = jnp.sum(x_ref[...], axis=0)
    o_ref[...] = jnp.broadcast_to(total[None], o_ref.shape)


def sent(blocks, axes):
    return lax.all_to_all(blocks, axes, 0, 0, tiled=True)


def spread(arrived, count):
    again = shape((count, *arrived.shape[1:]))
    return call(spread_kernel, again)(arrived)


def all_sum(parts, axes):
    size = lax.axis_size(axes)
    lines = parts.shape[0] * parts.shape[1] // size
    arrived = sent(parts.reshape(size, lines, LANES), axes)
    return sent(spread(arrived, size), axes).reshape(parts.shape)


def ring_sum(parts, outer, inner):
    count = lax.axis_size(outer)
    lines = parts.shape[0] * parts.shape[1] // count
    arrived = sent(parts.reshape(count, lines, LANES), outer)
    arrived = sent(spread(arrived, lax.axis_size(inner)), inner)
    return sent(spread(arrived, count), outer).reshape(parts.shape)


def side_by_side(ref, count):
    return jnp.concatenate([ref[i] for i in range(count)], axis=1)


def store_right(left, high, low, out_ref):
    blocks = high.shape[1] // LANES
    left_pieces = stacked(left)
    right = folded(mxu(left_pieces, high, NN) + mxu(left_pieces, low, NN))
    right = right * (1.0 / REPLICAS)
    for i in range(blocks):
        out_ref[i] = right[:, i * LANES : (i + 1) * LANES]
    gram = exact(left, left, NT) * (1.0 / GRAM_COPIES)
    out_ref[blocks] = jnp.concatenate([gram, jnp.zeros_like(gram)], axis=1)


def halve_kernel(mine_ref, came_ref, high_ref, low_ref):
    high_ref[...], low_ref[...] = pieces(mine_ref[...] + came_ref[...])


def halve(mine, came):
    outs = (shape(mine.shape, bf16), shape(mine.shape, bf16))
    cost = pl.CostEstimate(
        flops=3 * mine.size, bytes_accessed=12 * mine.size, transcendentals=0
    )
    block = pl.BlockSpec((TALL, mine.shape[1]), lambda i: (i, 0))
    return call(
        halve_kernel,
        outs,
        grid=(mine.shape[0] // TALL,),
        in_specs=[block, block],
        out_specs=[block, block],
        cost_estimate=cost,
    )(streamed(mine), streamed(came))


def first_right_kernel(left_ref, high_ref, low_ref, out_ref):
    left = side_by_side(left_ref, left_ref.shape[0])
    store_right(left, high_ref[...], low_ref[...], out_ref)


def first_right(left, high, low):
    outs = shape((high.shape[1] // LANES + 1, R, LANES))
    return call(first_right_kernel, outs)(left, high, low)


def left_kernel(right_ref, high_ref, low_ref, out_ref):
    blocks = right_ref.shape[0] - 1
    right = stacked(side_by_side(right_ref, blocks))
    left = mxu(right, high_ref[...], NT) + mxu(right, low_ref[...], NT)
    left = folded(left) * (1.0 / REPLICAS)
    for i in range(out_ref.shape[0]):
        out_ref[i] = left[:, i * LANES : (i + 1) * LANES]


def left_part(right, high, low):
    outs = shape((high.shape[0] // LANES, R, LANES))
    return call(left_kernel, outs)(right, high, low)


def second_right_kernel(
    inverse_ref, raw_ref, high_ref, low_ref, out_ref, left_ref
):
    raw = side_by_side(raw_ref, raw_ref.shape[0])
    left = exact(inverse_ref[...], raw, NN)
    left_ref[...] = left
    store_right(left, high_ref[...], low_ref[...], out_ref)


def second_right(inverse, raw, high, low):
    rows, cols = high.shape
    outs = (shape((cols // LANES + 1, R, LANES)), shape((R, rows)))
    return call(second_right_kernel, outs)(inverse, raw, high, low)


def lower_inverse(gram):
    row = lax.broadcasted_iota(jnp.int32, (R, R), 0)
    column = lax.broadcasted_iota(jnp.int32, (R, R), 1)
    work = jnp.concatenate([gram, (row == column).astype(f32)], axis=1)
    bands = [work[8 * i : 8 * i + 8] for i in range(R // 8)]
    below = lax.broadcasted_iota(jnp.int32, (8, LANES), 0)
    scales = []
    for p in range(R // 8):
        live = range(p, R // 8)
        spread = {
            i: [
                jnp.broadcast_to(bands[i][:, 8 * p + c : 8 * p + c + 1], (8, LANES))
                for c in range(8)
            ]
            for i in live
        }
        for k in range(8):
            pivot_row = bands[p][k : k + 1]
            pivots = [spread[p][c][k : k + 1] for c in range(8)]
            scales.append(lax.rsqrt(pivots[k]))
            inverse = 1.0 / pivots[k]
            for i in live:
                factor = spread[i][k] * inverse
                if i == p:
                    factor = jnp.where(below > k, factor, 0.0)
                for c in range(k + 1, 8):
                    spread[i][c] = spread[i][c] - factor * pivots[c]
                bands[i] = bands[i] - factor * pivot_row
    out = []
    for i in range(R // 8):
        scale = jnp.concatenate(scales[8 * i : 8 * i + 8], axis=0)
        out.append(bands[i][:, R:] * scale[:, R:])
    return jnp.concatenate(out, axis=0)


def inverse_kernel(right_ref, out_ref):
    out_ref[...] = lower_inverse(right_ref[0][:, :R])


def last_block(right):
    last = right.shape[0] - 1
    return pl.BlockSpec((1, R, LANES), lambda i: (last, 0, 0))


def inverse_of(right):
    return call(
        inverse_kernel,
        shape((R, R)),
        grid=(1,),
        in_specs=[last_block(right)],
        out_specs=pl.BlockSpec((R, R), lambda i: (0, 0)),
    )(right)


def basis_kernel(right_ref, left_ref, inverse_ref, basis_ref, factor_ref):
    inverse = lower_inverse(right_ref[0][:, :R])
    inverse_ref[...] = inverse
    basis = exact(inverse, left_ref[...], NN)
    factor_ref[...] = (basis * math.sqrt(D)).astype(bf16)
    basis_ref[...] = across(basis.T)


def basis_of(right, left):
    rows = left.shape[1]
    whole = lambda i: (0, 0)
    return call(
        basis_kernel,
        (shape((R, R)), shape((rows, 4 * R), bf16), shape((R, rows), bf16)),
        grid=(1,),
        in_specs=[last_block(right), pl.BlockSpec((R, rows), whole)],
        out_specs=[
            pl.BlockSpec((R, R), whole),
            pl.BlockSpec((rows, 4 * R), whole),
            pl.BlockSpec((R, rows), whole),
        ],
    )(right, left)


def error_kernel(
    core_ref, inverse_ref, own_ref, came_ref, basis_ref, p_ref, x_ref, g_ref, e_ref,
    new_ref, p_out_ref, q_out_ref, held_ref, done_ref, q_ref, sent_sem,
):
    count, _, step = done_ref.shape
    copies = []

    def leave(source, target):
        copies.append(pltpu.make_async_copy(source, target, sent_sem.at[len(copies)]))
        copies[-1].start()

    leave(p_ref, p_out_ref)
    width = g_ref.shape[1] // 2
    inverse = across(inverse_ref[...])
    for half, raw_ref in enumerate((own_ref, came_ref)):
        start = lax.rem(core_ref[0] + half, 2) * width
        columns = pl.ds(pl.multiple_of(start, LANES), width)
        raw = side_by_side(raw_ref, raw_ref.shape[0] - 1)
        right = mxu(inverse, down(raw), NN)
        q_ref[:, columns] = right.astype(bf16)
        held_ref[:, columns] = down(right)
    leave(q_ref, q_out_ref)
    turned = x_ref[...].T
    for i in range(count):
        columns = pl.ds(i * step, step)
        merged = mxu(turned, g_ref[:, columns], NN) + e_ref[0, :, columns].astype(f32)
        approximation = mxu(basis_ref[...], held_ref[:, columns], NN)
        done_ref[i] = (merged - approximation).astype(bf16)
        leave(done_ref.at[i], new_ref.at[0, :, columns])
    for copy in copies:
        copy.wait()


def final(core, inverse, own, came, basis, p_factor, inputs, out_grads, error):
    rows = inputs.shape[1]
    cols = out_grads.shape[1]
    step = 2 * LANES
    count = cols // step
    vmem = pl.BlockSpec(memory_space=pltpu.VMEM)
    outs = (shape(error.shape, bf16), shape((R, rows), bf16), shape((R, cols), bf16))
    return call(
        error_kernel,
        outs,
        in_specs=[pl.BlockSpec(memory_space=pltpu.SMEM)] + [vmem] * 8,
        out_specs=[pl.BlockSpec(memory_space=pltpu.HBM)] * 3,
        scratch_shapes=[
            pltpu.VMEM((4 * R, cols), bf16),
            pltpu.VMEM((count, rows, step), bf16),
            pltpu.VMEM((R, cols), bf16),
            pltpu.SemaphoreType.DMA((count + 2,)),
        ],
    )(core, inverse, own, came, basis, p_factor, inputs, out_grads, error)


def shards(inputs, out_grads, error, q_init):
    core = lax.axis_index("core").reshape(1)
    swap = [(0, 1), (1, 0)]
    part = first_left(inputs, out_grads, error, q_init)
    mine, other = merge(core, inputs, out_grads, error)
    came = lax.ppermute(other, "core", swap)
    left = ring_sum(part, XC, "z")
    high, low = halve(mine, came)
    right = all_sum(first_right(left, high, low), XY)
    inverse = inverse_of(right)
    raw = ring_sum(left_part(right, high, low), XC, "z")
    part, left = second_right(inverse, raw, high, low)
    own = all_sum(part, XY)
    came = lax.ppermute(own, "core", swap)
    inverse, basis, p_factor = basis_of(own, left)
    new_error, p_factor, q_factor = final(
        core, inverse, own, came, basis, p_factor, inputs, out_grads, error
    )
    return new_error, p_factor.T, q_factor.T


def solution(mesh):
    rep, fsdp, tp = mesh.devices.shape
    fine = Mesh(mesh.devices.reshape(rep // 2, 2, fsdp, tp), ("x", "core", "z", "y"))
    both = ("x", "core")
    in_specs = (P(both, "y"), P(both, "z"), P(both, "y", "z"), P("z", None))
    out_specs = (P(both, "y", "z"), P("y", None), P("z", None))
    return jax.shard_map(
        shards, mesh=fine, in_specs=in_specs, out_specs=out_specs, check_vma=False
    )
```

```python
import functools
import math

import jax
import jax.numpy as jnp
from jax import lax
from jax.experimental import pallas as pl
from jax.experimental.pallas import tpu as pltpu
from jax.sharding import Mesh
from jax.sharding import PartitionSpec as P

D = 4096
R = 64
LANES = 128
GRAM_LINES = R * R // LANES
TALL = 256
REPLICAS = 8
XC = ("x", "core")
XY = ("x", "y")
GRAM_COPIES = 4

f32 = jnp.float32
bf16 = jnp.bfloat16
NN = (((1,), (0,)), ((), ()))
NT = (((1,), (1,)), ((), ()))
TN = (((0,), (0,)), ((), ()))


def mxu(a, b, dims):
    return lax.dot_general(a, b, dims, preferred_element_type=f32)


def exact(a, b, dims):
    return lax.dot_general(
        a, b, dims, precision=lax.Precision.HIGHEST, preferred_element_type=f32
    )


def pieces(x):
    high = x.astype(bf16)
    return high, (x - high.astype(f32)).astype(bf16)


def stacked(x):
    return jnp.concatenate(pieces(x), axis=0)


def folded(x):
    return x[:R] + x[R:]


def across(a):
    high, low = pieces(a)
    return jnp.concatenate([high, high, low, low], axis=1)


def down(b):
    high, low = pieces(b)
    return jnp.concatenate([high, low, high, low], axis=0)


def call(kernel, out_shape, **kw):
    params = pltpu.CompilerParams(vmem_limit_bytes=kw.pop("vmem", 12 << 20))
    return pl.pallas_call(kernel, out_shape=out_shape, compiler_params=params, **kw)


def streamed(x):
    return pltpu.with_memory_space_constraint(x, pltpu.HBM)


def shape(s, dtype=f32):
    return jax.ShapeDtypeStruct(s, dtype)


def times_q(a, q_ref):
    half = a.shape[1] // 2
    parts = [
        mxu(a[:, part], q_ref[:, part], NT) for part in (slice(half), slice(half, None))
    ]
    return (parts[0] + parts[1]).T


def first_left_kernel(
    x_hbm, g_hbm, e_hbm, q_hbm, part_ref, x_ref, g_ref, e_ref, q_ref, here
):
    rows = e_ref.shape[0]
    pairs = [(q_hbm, q_ref), (g_hbm, g_ref), (x_hbm, x_ref)]
    for at in range(0, rows, TALL):
        lines = pl.ds(at, TALL)
        pairs.append((e_hbm.at[0, lines], e_ref.at[lines]))
    copies = [
        pltpu.make_async_copy(source, target, here.at[i])
        for i, (source, target) in enumerate(pairs)
    ]
    for copy in copies:
        copy.start()
    copies[0].wait()
    copies[1].wait()
    through = stacked(times_q(g_ref[...], q_ref))
    copies[2].wait()
    left = folded(mxu(through, x_ref[...], NN))
    for i, at in enumerate(range(0, rows, TALL)):
        lines = slice(at, at + TALL)
        copies[3 + i].wait()
        part = (times_q(e_ref[lines], q_ref) + left[:, lines]) * (1.0 / REPLICAS)
        for j in range(TALL // LANES):
            block = part[:, j * LANES : (j + 1) * LANES]
            part_ref[at // LANES + j] = block


def first_left(inputs, out_grads, error, q_init):
    rows = inputs.shape[1]
    operands = (inputs, out_grads, error, q_init.T)
    held = [pltpu.VMEM(a.shape[-2:], bf16) for a in operands]
    return call(
        first_left_kernel,
        shape((rows // LANES, R, LANES)),
        in_specs=[pl.BlockSpec(memory_space=pltpu.HBM)] * 4,
        out_specs=pl.BlockSpec(memory_space=pltpu.VMEM),
        scratch_shapes=held + [pltpu.SemaphoreType.DMA((3 + rows // TALL,))],
    )(*(streamed(a) for a in operands))


def merge_kernel(core_ref, x_ref, g_ref, e_ref, mine_ref, other_ref):
    merged = mxu(x_ref[...], g_ref[...], TN) + e_ref[0].astype(f32)
    half = merged.shape[1] // 2

    @pl.when(core_ref[0] == 0)
    def _():
        mine_ref[...] = merged[:, :half]
        other_ref[...] = merged[:, half:]

    @pl.when(core_ref[0] != 0)
    def _():
        mine_ref[...] = merged[:, half:]
        other_ref[...] = merged[:, :half]


def merge(core, inputs, out_grads, error):
    tokens, rows = inputs.shape
    cols = out_grads.shape[1]
    half = pl.BlockSpec((TALL, cols // 2), lambda i, c: (i, 0))
    spec = pltpu.PrefetchScalarGridSpec(
        num_scalar_prefetch=1,
        grid=(rows // TALL,),
        in_specs=[
            pl.BlockSpec((tokens, TALL), lambda i, c: (0, i)),
            pl.BlockSpec((tokens, cols), lambda i, c: (0, 0)),
            pl.BlockSpec((1, TALL, cols), lambda i, c: (0, i, 0)),
        ],
        out_specs=[half, half],
    )
    outs = (pltpu.HBM((rows, cols // 2), f32), pltpu.HBM((rows, cols // 2), f32))
    cost = pl.CostEstimate(
        flops=2 * tokens * rows * cols, bytes_accessed=12 * rows * cols, transcendentals=0
    )
    return call(merge_kernel, outs, grid_spec=spec, cost_estimate=cost)(
        core, *(streamed(a) for a in (inputs, out_grads, error))
    )


def spread_kernel(x_ref, o_ref):
    total = jnp.sum(x_ref[...], axis=0)
    o_ref[...] = jnp.broadcast_to(total[None], o_ref.shape)


def sent(blocks, axes):
    return lax.all_to_all(blocks, axes, 0, 0, tiled=True)


def spread(arrived, count):
    again = shape((count, *arrived.shape[1:]))
    return call(spread_kernel, again)(arrived)


def packed_kernel(count, x_ref, o_ref):
    lines = x_ref.shape[0] // count
    total = x_ref[:lines]
    for i in range(1, count):
        total = total + x_ref[i * lines : (i + 1) * lines]
    for i in range(count):
        o_ref[i * lines : (i + 1) * lines] = total


def all_sum(parts, axes):
    size = lax.axis_size(axes)
    rows = (size, 1, parts.size // size)
    arrived = sent(parts.reshape(rows), axes).reshape(parts.shape)
    kernel = functools.partial(packed_kernel, size)
    again = call(kernel, shape(parts.shape))(arrived)
    return sent(again.reshape(rows), axes).reshape(parts.shape)


def ring_sum(parts, outer, inner):
    count = lax.axis_size(outer)
    lines = parts.shape[0] * parts.shape[1] // count
    arrived = sent(parts.reshape(count, lines, LANES), outer)
    arrived = sent(spread(arrived, lax.axis_size(inner)), inner)
    return sent(spread(arrived, count), outer).reshape(parts.shape)


def side_by_side(ref, count):
    return jnp.concatenate([ref[i] for i in range(count)], axis=1)


def right_lines(cols):
    return cols // LANES * R + GRAM_LINES, LANES


def right_of(ref):
    blocks = ref.shape[0] // R
    return jnp.concatenate([ref[i * R : (i + 1) * R] for i in range(blocks)], axis=1)


def gram_of(ref):
    lines = ref[...]
    return jnp.concatenate([lines[:, :R], lines[:, R:]], axis=0)


def store_right(left, high, low, out_ref):
    blocks = high.shape[1] // LANES
    left_pieces = stacked(left)
    right = folded(mxu(left_pieces, high, NN) + mxu(left_pieces, low, NN))
    right = right * (1.0 / REPLICAS)
    for i in range(blocks):
        out_ref[i * R : (i + 1) * R] = right[:, i * LANES : (i + 1) * LANES]
    gram = exact(left, left, NT) * (1.0 / GRAM_COPIES)
    out_ref[blocks * R :] = jnp.concatenate(
        [gram[:GRAM_LINES], gram[GRAM_LINES:]], axis=1
    )


def halve_kernel(mine_ref, came_ref, high_ref, low_ref):
    high_ref[...], low_ref[...] = pieces(mine_ref[...] + came_ref[...])


def halve(mine, came):
    outs = (shape(mine.shape, bf16), shape(mine.shape, bf16))
    cost = pl.CostEstimate(
        flops=3 * mine.size, bytes_accessed=12 * mine.size, transcendentals=0
    )
    block = pl.BlockSpec((TALL, mine.shape[1]), lambda i: (i, 0))
    return call(
        halve_kernel,
        outs,
        grid=(mine.shape[0] // TALL,),
        in_specs=[block, block],
        out_specs=[block, block],
        cost_estimate=cost,
    )(streamed(mine), streamed(came))


def first_right_kernel(left_ref, high_ref, low_ref, out_ref):
    left = side_by_side(left_ref, left_ref.shape[0])
    store_right(left, high_ref[...], low_ref[...], out_ref)


def first_right(left, high, low):
    outs = shape(right_lines(high.shape[1]))
    return call(first_right_kernel, outs)(left, high, low)


def left_kernel(right_ref, high_ref, low_ref, out_ref):
    right = stacked(right_of(right_ref))
    left = mxu(right, high_ref[...], NT) + mxu(right, low_ref[...], NT)
    left = folded(left) * (1.0 / REPLICAS)
    for i in range(out_ref.shape[0]):
        out_ref[i] = left[:, i * LANES : (i + 1) * LANES]


def left_part(right, high, low):
    outs = shape((high.shape[0] // LANES, R, LANES))
    return call(left_kernel, outs)(right, high, low)


def second_right_kernel(
    inverse_ref, raw_ref, high_ref, low_ref, out_ref, left_ref
):
    raw = side_by_side(raw_ref, raw_ref.shape[0])
    left = exact(inverse_ref[...], raw, NN)
    left_ref[...] = left
    store_right(left, high_ref[...], low_ref[...], out_ref)


def second_right(inverse, raw, high, low):
    rows, cols = high.shape
    outs = (shape(right_lines(cols)), shape((R, rows)))
    return call(second_right_kernel, outs)(inverse, raw, high, low)


def lower_inverse(gram):
    row = lax.broadcasted_iota(jnp.int32, (R, R), 0)
    column = lax.broadcasted_iota(jnp.int32, (R, R), 1)
    work = jnp.concatenate([gram, (row == column).astype(f32)], axis=1)
    bands = [work[8 * i : 8 * i + 8] for i in range(R // 8)]
    below = lax.broadcasted_iota(jnp.int32, (8, LANES), 0)
    scales = []
    for p in range(R // 8):
        live = range(p, R // 8)
        spread = {
            i: [
                jnp.broadcast_to(bands[i][:, 8 * p + c : 8 * p + c + 1], (8, LANES))
                for c in range(8)
            ]
            for i in live
        }
        for k in range(8):
            pivot_row = bands[p][k : k + 1]
            pivots = [spread[p][c][k : k + 1] for c in range(8)]
            scales.append(lax.rsqrt(pivots[k]))
            inverse = 1.0 / pivots[k]
            for i in live:
                factor = spread[i][k] * inverse
                if i == p:
                    factor = jnp.where(below > k, factor, 0.0)
                for c in range(k + 1, 8):
                    spread[i][c] = spread[i][c] - factor * pivots[c]
                bands[i] = bands[i] - factor * pivot_row
    out = []
    for i in range(R // 8):
        scale = jnp.concatenate(scales[8 * i : 8 * i + 8], axis=0)
        out.append(bands[i][:, R:] * scale[:, R:])
    return jnp.concatenate(out, axis=0)


def inverse_kernel(right_ref, out_ref):
    out_ref[...] = lower_inverse(gram_of(right_ref))


def last_block(right):
    last = right.shape[0] // GRAM_LINES - 1
    return pl.BlockSpec((GRAM_LINES, LANES), lambda i: (last, 0))


def inverse_of(right):
    return call(
        inverse_kernel,
        shape((R, R)),
        grid=(1,),
        in_specs=[last_block(right)],
        out_specs=pl.BlockSpec((R, R), lambda i: (0, 0)),
    )(right)


def basis_kernel(right_ref, left_ref, inverse_ref, basis_ref, factor_ref):
    inverse = lower_inverse(gram_of(right_ref))
    inverse_ref[...] = inverse
    basis = exact(inverse, left_ref[...], NN)
    factor_ref[...] = (basis * math.sqrt(D)).astype(bf16)
    basis_ref[...] = across(basis.T)


def basis_of(right, left):
    rows = left.shape[1]
    whole = lambda i: (0, 0)
    return call(
        basis_kernel,
        (shape((R, R)), shape((rows, 4 * R), bf16), shape((R, rows), bf16)),
        grid=(1,),
        in_specs=[last_block(right), pl.BlockSpec((R, rows), whole)],
        out_specs=[
            pl.BlockSpec((R, R), whole),
            pl.BlockSpec((rows, 4 * R), whole),
            pl.BlockSpec((R, rows), whole),
        ],
    )(right, left)


def error_kernel(
    core_ref, inverse_ref, own_ref, came_ref, basis_ref, p_ref, x_ref, g_ref, e_ref,
    new_ref, p_out_ref, q_out_ref, held_ref, done_ref, q_ref, sent_sem,
):
    count, _, step = done_ref.shape
    copies = []

    def leave(source, target):
        copies.append(pltpu.make_async_copy(source, target, sent_sem.at[len(copies)]))
        copies[-1].start()

    leave(p_ref, p_out_ref)
    width = g_ref.shape[1] // 2
    inverse = across(inverse_ref[...])
    for half, raw_ref in enumerate((own_ref, came_ref)):
        start = lax.rem(core_ref[0] + half, 2) * width
        columns = pl.ds(pl.multiple_of(start, LANES), width)
        raw = right_of(raw_ref)
        right = mxu(inverse, down(raw), NN)
        q_ref[:, columns] = right.astype(bf16)
        held_ref[:, columns] = down(right)
    leave(q_ref, q_out_ref)
    turned = x_ref[...].T
    for i in range(count):
        columns = pl.ds(i * step, step)
        merged = mxu(turned, g_ref[:, columns], NN) + e_ref[0, :, columns].astype(f32)
        approximation = mxu(basis_ref[...], held_ref[:, columns], NN)
        done_ref[i] = (merged - approximation).astype(bf16)
        leave(done_ref.at[i], new_ref.at[0, :, columns])
    for copy in copies:
        copy.wait()


def final(core, inverse, own, came, basis, p_factor, inputs, out_grads, error):
    rows = inputs.shape[1]
    cols = out_grads.shape[1]
    step = 2 * LANES
    count = cols // step
    vmem = pl.BlockSpec(memory_space=pltpu.VMEM)
    outs = (shape(error.shape, bf16), shape((R, rows), bf16), shape((R, cols), bf16))
    return call(
        error_kernel,
        outs,
        in_specs=[pl.BlockSpec(memory_space=pltpu.SMEM)] + [vmem] * 8,
        out_specs=[pl.BlockSpec(memory_space=pltpu.HBM)] * 3,
        scratch_shapes=[
            pltpu.VMEM((4 * R, cols), bf16),
            pltpu.VMEM((count, rows, step), bf16),
            pltpu.VMEM((R, cols), bf16),
            pltpu.SemaphoreType.DMA((count + 2,)),
        ],
    )(core, inverse, own, came, basis, p_factor, inputs, out_grads, error)


def shards(inputs, out_grads, error, q_init):
    core = lax.axis_index("core").reshape(1)
    swap = [(0, 1), (1, 0)]
    part = first_left(inputs, out_grads, error, q_init)
    mine, other = merge(core, inputs, out_grads, error)
    came = lax.ppermute(other, "core", swap)
    left = ring_sum(part, XC, "z")
    high, low = halve(mine, came)
    right = all_sum(first_right(left, high, low), XY)
    inverse = inverse_of(right)
    raw = ring_sum(left_part(right, high, low), XC, "z")
    part, left = second_right(inverse, raw, high, low)
    own = all_sum(part, XY)
    came = lax.ppermute(own, "core", swap)
    inverse, basis, p_factor = basis_of(own, left)
    new_error, p_factor, q_factor = final(
        core, inverse, own, came, basis, p_factor, inputs, out_grads, error
    )
    return new_error, p_factor.T, q_factor.T


def solution(mesh):
    rep, fsdp, tp = mesh.devices.shape
    fine = Mesh(mesh.devices.reshape(rep // 2, 2, fsdp, tp), ("x", "core", "z", "y"))
    both = ("x", "core")
    in_specs = (P(both, "y"), P(both, "z"), P(both, "y", "z"), P("z", None))
    out_specs = (P(both, "y", "z"), P("y", None), P("z", None))
    return jax.shard_map(
        shards, mesh=fine, in_specs=in_specs, out_specs=out_specs, check_vma=False
    )
```

```python
import functools
import math

import jax
import jax.numpy as jnp
from jax import lax
from jax.experimental import pallas as pl
from jax.experimental.pallas import tpu as pltpu
from jax.sharding import Mesh
from jax.sharding import PartitionSpec as P

D = 4096
R = 64
LANES = 128
GRAM_LINES = R * R // LANES
TALL = 256
REPLICAS = 8
XC = ("x", "core")
XY = ("x", "y")
GRAM_COPIES = 4

f32 = jnp.float32
bf16 = jnp.bfloat16
NN = (((1,), (0,)), ((), ()))
NT = (((1,), (1,)), ((), ()))
TN = (((0,), (0,)), ((), ()))


def mxu(a, b, dims):
    return lax.dot_general(a, b, dims, preferred_element_type=f32)


def pieces(x):
    high = x.astype(bf16)
    return high, (x - high.astype(f32)).astype(bf16)


def thirds(x):
    high = x.astype(bf16)
    rest = x - high.astype(f32)
    middle = rest.astype(bf16)
    return high, middle, (rest - middle.astype(f32)).astype(bf16)


def exact(a, b):
    ah, am, al = thirds(a)
    bh, bm, bl = thirds(b)
    left = jnp.concatenate([ah, ah, am, am, ah, al], axis=1)
    right = jnp.concatenate([bh, bm, bh, bm, bl, bh], axis=0)
    return mxu(left, right, NN)


def gram(x):
    rows = jnp.concatenate(thirds(x), axis=0)
    terms = mxu(rows, rows, NT)
    terms = terms[2 * R :] + terms[R : 2 * R] + terms[:R]
    return terms[:, 2 * R :] + terms[:, R : 2 * R] + terms[:, :R]


def stacked(x):
    return jnp.concatenate(pieces(x), axis=0)


def folded(x):
    return x[:R] + x[R:]


def across(a):
    high, low = pieces(a)
    return jnp.concatenate([high, high, low, low], axis=1)


def down(b):
    high, low = pieces(b)
    return jnp.concatenate([high, low, high, low], axis=0)


def call(kernel, out_shape, **kw):
    params = pltpu.CompilerParams(vmem_limit_bytes=kw.pop("vmem", 12 << 20))
    return pl.pallas_call(kernel, out_shape=out_shape, compiler_params=params, **kw)


def streamed(x):
    return pltpu.with_memory_space_constraint(x, pltpu.HBM)


def shape(s, dtype=f32):
    return jax.ShapeDtypeStruct(s, dtype)


def times_q(a, q_ref):
    half = a.shape[1] // 2
    parts = [
        mxu(a[:, part], q_ref[:, part], NT) for part in (slice(half), slice(half, None))
    ]
    return (parts[0] + parts[1]).T


def first_left_kernel(
    x_hbm, g_hbm, e_hbm, q_hbm, part_ref, x_ref, g_ref, e_ref, q_ref, here
):
    rows = e_ref.shape[0]
    pairs = [(q_hbm, q_ref), (g_hbm, g_ref), (x_hbm, x_ref)]
    for at in range(0, rows, TALL):
        lines = pl.ds(at, TALL)
        pairs.append((e_hbm.at[0, lines], e_ref.at[lines]))
    copies = [
        pltpu.make_async_copy(source, target, here.at[i])
        for i, (source, target) in enumerate(pairs)
    ]
    for copy in copies:
        copy.start()
    copies[0].wait()
    copies[1].wait()
    through = stacked(times_q(g_ref[...], q_ref))
    copies[2].wait()
    left = folded(mxu(through, x_ref[...], NN))
    for i, at in enumerate(range(0, rows, TALL)):
        lines = slice(at, at + TALL)
        copies[3 + i].wait()
        part = (times_q(e_ref[lines], q_ref) + left[:, lines]) * (1.0 / REPLICAS)
        for j in range(TALL // LANES):
            block = part[:, j * LANES : (j + 1) * LANES]
            part_ref[at // LANES + j] = block


def first_left(inputs, out_grads, error, q_init):
    rows = inputs.shape[1]
    operands = (inputs, out_grads, error, q_init.T)
    held = [pltpu.VMEM(a.shape[-2:], bf16) for a in operands]
    return call(
        first_left_kernel,
        shape((rows // LANES, R, LANES)),
        in_specs=[pl.BlockSpec(memory_space=pltpu.HBM)] * 4,
        out_specs=pl.BlockSpec(memory_space=pltpu.VMEM),
        scratch_shapes=held + [pltpu.SemaphoreType.DMA((3 + rows // TALL,))],
    )(*(streamed(a) for a in operands))


def merge_kernel(core_ref, x_ref, g_ref, e_ref, mine_ref, other_ref):
    merged = mxu(x_ref[...], g_ref[...], TN) + e_ref[0].astype(f32)
    half = merged.shape[1] // 2

    @pl.when(core_ref[0] == 0)
    def _():
        mine_ref[...] = merged[:, :half]
        other_ref[...] = merged[:, half:]

    @pl.when(core_ref[0] != 0)
    def _():
        mine_ref[...] = merged[:, half:]
        other_ref[...] = merged[:, :half]


def merge(core, inputs, out_grads, error):
    tokens, rows = inputs.shape
    cols = out_grads.shape[1]
    half = pl.BlockSpec((TALL, cols // 2), lambda i, c: (i, 0))
    spec = pltpu.PrefetchScalarGridSpec(
        num_scalar_prefetch=1,
        grid=(rows // TALL,),
        in_specs=[
            pl.BlockSpec((tokens, TALL), lambda i, c: (0, i)),
            pl.BlockSpec((tokens, cols), lambda i, c: (0, 0)),
            pl.BlockSpec((1, TALL, cols), lambda i, c: (0, i, 0)),
        ],
        out_specs=[half, half],
    )
    outs = (pltpu.HBM((rows, cols // 2), f32), pltpu.HBM((rows, cols // 2), f32))
    cost = pl.CostEstimate(
        flops=2 * tokens * rows * cols, bytes_accessed=12 * rows * cols, transcendentals=0
    )
    return call(merge_kernel, outs, grid_spec=spec, cost_estimate=cost)(
        core, *(streamed(a) for a in (inputs, out_grads, error))
    )


def spread_kernel(x_ref, o_ref):
    total = jnp.sum(x_ref[...], axis=0)
    o_ref[...] = jnp.broadcast_to(total[None], o_ref.shape)


def sent(blocks, axes):
    return lax.all_to_all(blocks, axes, 0, 0, tiled=True)


def spread(arrived, count):
    again = shape((count, *arrived.shape[1:]))
    return call(spread_kernel, again)(arrived)


def packed_kernel(count, x_ref, o_ref):
    lines = x_ref.shape[0] // count
    total = x_ref[:lines]
    for i in range(1, count):
        total = total + x_ref[i * lines : (i + 1) * lines]
    for i in range(count):
        o_ref[i * lines : (i + 1) * lines] = total


def all_sum(parts, axes):
    size = lax.axis_size(axes)
    rows = (size, 1, parts.size // size)
    arrived = sent(parts.reshape(rows), axes).reshape(parts.shape)
    kernel = functools.partial(packed_kernel, size)
    again = call(kernel, shape(parts.shape))(arrived)
    return sent(again.reshape(rows), axes).reshape(parts.shape)


def ring_sum(parts, outer, inner):
    count = lax.axis_size(outer)
    lines = parts.shape[0] * parts.shape[1] // count
    arrived = sent(parts.reshape(count, lines, LANES), outer)
    arrived = sent(spread(arrived, lax.axis_size(inner)), inner)
    return sent(spread(arrived, count), outer).reshape(parts.shape)


def side_by_side(ref, count):
    return jnp.concatenate([ref[i] for i in range(count)], axis=1)


def right_lines(cols):
    return cols // LANES * R + GRAM_LINES, LANES


def right_of(ref):
    blocks = ref.shape[0] // R
    return jnp.concatenate([ref[i * R : (i + 1) * R] for i in range(blocks)], axis=1)


def gram_of(ref):
    lines = ref[...]
    return jnp.concatenate([lines[:, :R], lines[:, R:]], axis=0)


def store_right(left, high, low, out_ref):
    blocks = high.shape[1] // LANES
    left_pieces = stacked(left)
    right = folded(mxu(left_pieces, high, NN) + mxu(left_pieces, low, NN))
    right = right * (1.0 / REPLICAS)
    for i in range(blocks):
        out_ref[i * R : (i + 1) * R] = right[:, i * LANES : (i + 1) * LANES]
    part = gram(left) * (1.0 / GRAM_COPIES)
    out_ref[blocks * R :] = jnp.concatenate(
        [part[:GRAM_LINES], part[GRAM_LINES:]], axis=1
    )


def halve_kernel(mine_ref, came_ref, high_ref, low_ref):
    high_ref[...], low_ref[...] = pieces(mine_ref[...] + came_ref[...])


def halve(mine, came):
    outs = (shape(mine.shape, bf16), shape(mine.shape, bf16))
    cost = pl.CostEstimate(
        flops=3 * mine.size, bytes_accessed=12 * mine.size, transcendentals=0
    )
    block = pl.BlockSpec((TALL, mine.shape[1]), lambda i: (i, 0))
    return call(
        halve_kernel,
        outs,
        grid=(mine.shape[0] // TALL,),
        in_specs=[block, block],
        out_specs=[block, block],
        cost_estimate=cost,
    )(streamed(mine), streamed(came))


def first_right_kernel(left_ref, high_ref, low_ref, out_ref):
    left = side_by_side(left_ref, left_ref.shape[0])
    store_right(left, high_ref[...], low_ref[...], out_ref)


def first_right(left, high, low):
    outs = shape(right_lines(high.shape[1]))
    return call(first_right_kernel, outs)(left, high, low)


def left_kernel(right_ref, high_ref, low_ref, out_ref):
    right = stacked(right_of(right_ref))
    left = mxu(right, high_ref[...], NT) + mxu(right, low_ref[...], NT)
    left = folded(left) * (1.0 / REPLICAS)
    for i in range(out_ref.shape[0]):
        out_ref[i] = left[:, i * LANES : (i + 1) * LANES]


def left_part(right, high, low):
    outs = shape((high.shape[0] // LANES, R, LANES))
    return call(left_kernel, outs)(right, high, low)


def second_right_kernel(
    inverse_ref, raw_ref, high_ref, low_ref, out_ref, left_ref
):
    raw = side_by_side(raw_ref, raw_ref.shape[0])
    left = exact(inverse_ref[...], raw)
    left_ref[...] = left
    store_right(left, high_ref[...], low_ref[...], out_ref)


def second_right(inverse, raw, high, low):
    rows, cols = high.shape
    outs = (shape(right_lines(cols)), shape((R, rows)))
    return call(second_right_kernel, outs)(inverse, raw, high, low)


def lower_inverse(gram):
    row = lax.broadcasted_iota(jnp.int32, (R, R), 0)
    column = lax.broadcasted_iota(jnp.int32, (R, R), 1)
    work = jnp.concatenate([gram, (row == column).astype(f32)], axis=1)
    bands = [work[8 * i : 8 * i + 8] for i in range(R // 8)]
    below = lax.broadcasted_iota(jnp.int32, (8, LANES), 0)
    scales = []
    for p in range(R // 8):
        live = range(p, R // 8)
        spread = {
            i: [
                jnp.broadcast_to(bands[i][:, 8 * p + c : 8 * p + c + 1], (8, LANES))
                for c in range(8)
            ]
            for i in live
        }
        for k in range(8):
            pivot_row = bands[p][k : k + 1]
            pivots = [spread[p][c][k : k + 1] for c in range(8)]
            scales.append(lax.rsqrt(pivots[k]))
            inverse = 1.0 / pivots[k]
            for i in live:
                factor = spread[i][k] * inverse
                if i == p:
                    factor = jnp.where(below > k, factor, 0.0)
                for c in range(k + 1, 8):
                    spread[i][c] = spread[i][c] - factor * pivots[c]
                bands[i] = bands[i] - factor * pivot_row
    out = []
    for i in range(R // 8):
        scale = jnp.concatenate(scales[8 * i : 8 * i + 8], axis=0)
        out.append(bands[i][:, R:] * scale[:, R:])
    return jnp.concatenate(out, axis=0)


def inverse_kernel(right_ref, out_ref):
    out_ref[...] = lower_inverse(gram_of(right_ref))


def last_block(right):
    last = right.shape[0] // GRAM_LINES - 1
    return pl.BlockSpec((GRAM_LINES, LANES), lambda i: (last, 0))


def inverse_of(right):
    return call(
        inverse_kernel,
        shape((R, R)),
        grid=(1,),
        in_specs=[last_block(right)],
        out_specs=pl.BlockSpec((R, R), lambda i: (0, 0)),
    )(right)


def basis_kernel(right_ref, left_ref, inverse_ref, basis_ref, factor_ref):
    inverse = lower_inverse(gram_of(right_ref))
    inverse_ref[...] = inverse
    basis = exact(inverse, left_ref[...])
    factor_ref[...] = (basis * math.sqrt(D)).astype(bf16)
    basis_ref[...] = across(basis.T)


def basis_of(right, left):
    rows = left.shape[1]
    whole = lambda i: (0, 0)
    return call(
        basis_kernel,
        (shape((R, R)), shape((rows, 4 * R), bf16), shape((R, rows), bf16)),
        grid=(1,),
        in_specs=[last_block(right), pl.BlockSpec((R, rows), whole)],
        out_specs=[
            pl.BlockSpec((R, R), whole),
            pl.BlockSpec((rows, 4 * R), whole),
            pl.BlockSpec((R, rows), whole),
        ],
    )(right, left)


def error_kernel(
    core_ref, inverse_ref, own_ref, came_ref, basis_ref, p_ref, x_ref, g_ref, e_ref,
    new_ref, p_out_ref, q_out_ref, held_ref, done_ref, q_ref, sent_sem,
):
    count, _, step = done_ref.shape
    copies = []

    def leave(source, target):
        copies.append(pltpu.make_async_copy(source, target, sent_sem.at[len(copies)]))
        copies[-1].start()

    leave(p_ref, p_out_ref)
    width = g_ref.shape[1] // 2
    inverse = across(inverse_ref[...])
    for half, raw_ref in enumerate((own_ref, came_ref)):
        start = lax.rem(core_ref[0] + half, 2) * width
        columns = pl.ds(pl.multiple_of(start, LANES), width)
        raw = right_of(raw_ref)
        right = mxu(inverse, down(raw), NN)
        q_ref[:, columns] = right.astype(bf16)
        held_ref[:, columns] = down(right)
    leave(q_ref, q_out_ref)
    turned = x_ref[...].T
    for i in range(count):
        columns = pl.ds(i * step, step)
        merged = mxu(turned, g_ref[:, columns], NN) + e_ref[0, :, columns].astype(f32)
        approximation = mxu(basis_ref[...], held_ref[:, columns], NN)
        done_ref[i] = (merged - approximation).astype(bf16)
        leave(done_ref.at[i], new_ref.at[0, :, columns])
    for copy in copies:
        copy.wait()


def final(core, inverse, own, came, basis, p_factor, inputs, out_grads, error):
    rows = inputs.shape[1]
    cols = out_grads.shape[1]
    step = 2 * LANES
    count = cols // step
    vmem = pl.BlockSpec(memory_space=pltpu.VMEM)
    outs = (shape(error.shape, bf16), shape((R, rows), bf16), shape((R, cols), bf16))
    return call(
        error_kernel,
        outs,
        in_specs=[pl.BlockSpec(memory_space=pltpu.SMEM)] + [vmem] * 8,
        out_specs=[pl.BlockSpec(memory_space=pltpu.HBM)] * 3,
        scratch_shapes=[
            pltpu.VMEM((4 * R, cols), bf16),
            pltpu.VMEM((count, rows, step), bf16),
            pltpu.VMEM((R, cols), bf16),
            pltpu.SemaphoreType.DMA((count + 2,)),
        ],
    )(core, inverse, own, came, basis, p_factor, inputs, out_grads, error)


def shards(inputs, out_grads, error, q_init):
    core = lax.axis_index("core").reshape(1)
    swap = [(0, 1), (1, 0)]
    part = first_left(inputs, out_grads, error, q_init)
    mine, other = merge(core, inputs, out_grads, error)
    came = lax.ppermute(other, "core", swap)
    left = ring_sum(part, XC, "z")
    high, low = halve(mine, came)
    right = all_sum(first_right(left, high, low), XY)
    inverse = inverse_of(right)
    raw = ring_sum(left_part(right, high, low), XC, "z")
    part, left = second_right(inverse, raw, high, low)
    own = all_sum(part, XY)
    came = lax.ppermute(own, "core", swap)
    inverse, basis, p_factor = basis_of(own, left)
    new_error, p_factor, q_factor = final(
        core, inverse, own, came, basis, p_factor, inputs, out_grads, error
    )
    return new_error, p_factor.T, q_factor.T


def solution(mesh):
    rep, fsdp, tp = mesh.devices.shape
    fine = Mesh(mesh.devices.reshape(rep // 2, 2, fsdp, tp), ("x", "core", "z", "y"))
    both = ("x", "core")
    in_specs = (P(both, "y"), P(both, "z"), P(both, "y", "z"), P("z", None))
    out_specs = (P(both, "y", "z"), P("y", None), P("z", None))
    return jax.shard_map(
        shards, mesh=fine, in_specs=in_specs, out_specs=out_specs, check_vma=False
    )
```

```python
import functools
import math

import jax
import jax.numpy as jnp
from jax import lax
from jax.experimental import pallas as pl
from jax.experimental.pallas import tpu as pltpu
from jax.sharding import Mesh
from jax.sharding import PartitionSpec as P

D = 4096
R = 64
LANES = 128
GRAM_LINES = R * R // LANES
TALL = 256
REPLICAS = 8
XC = ("x", "core")
XY = ("x", "y")
GRAM_COPIES = 4

f32 = jnp.float32
bf16 = jnp.bfloat16
NN = (((1,), (0,)), ((), ()))
NT = (((1,), (1,)), ((), ()))
TN = (((0,), (0,)), ((), ()))


def mxu(a, b, dims):
    return lax.dot_general(a, b, dims, preferred_element_type=f32)


def pieces(x):
    high = x.astype(bf16)
    return high, (x - high.astype(f32)).astype(bf16)


def thirds(x):
    high = x.astype(bf16)
    rest = x - high.astype(f32)
    middle = rest.astype(bf16)
    return high, middle, (rest - middle.astype(f32)).astype(bf16)


def exact(a, b):
    ah, am, al = thirds(a)
    bh, bm, bl = thirds(b)
    left = jnp.concatenate([ah, ah, am, am, ah, al], axis=1)
    right = jnp.concatenate([bh, bm, bh, bm, bl, bh], axis=0)
    return mxu(left, right, NN)


def gram(x):
    rows = jnp.concatenate(thirds(x), axis=0)
    terms = mxu(rows, rows, NT)
    terms = terms[2 * R :] + terms[R : 2 * R] + terms[:R]
    return terms[:, 2 * R :] + terms[:, R : 2 * R] + terms[:, :R]


def stacked(x):
    return jnp.concatenate(pieces(x), axis=0)


def folded(x):
    return x[:R] + x[R:]


def across(a):
    high, low = pieces(a)
    return jnp.concatenate([high, high, low, low], axis=1)


def down(b):
    high, low = pieces(b)
    return jnp.concatenate([high, low, high, low], axis=0)


def call(kernel, out_shape, **kw):
    params = pltpu.CompilerParams(vmem_limit_bytes=kw.pop("vmem", 12 << 20))
    return pl.pallas_call(kernel, out_shape=out_shape, compiler_params=params, **kw)


def streamed(x):
    return pltpu.with_memory_space_constraint(x, pltpu.HBM)


def shape(s, dtype=f32):
    return jax.ShapeDtypeStruct(s, dtype)


def times_q(a, q_ref):
    half = a.shape[1] // 2
    parts = [
        mxu(a[:, part], q_ref[:, part], NT) for part in (slice(half), slice(half, None))
    ]
    return (parts[0] + parts[1]).T


def first_left_kernel(
    x_hbm, g_hbm, e_hbm, q_hbm, part_ref, x_ref, g_ref, e_ref, q_ref, here
):
    rows = e_ref.shape[0]
    pairs = [(q_hbm, q_ref), (g_hbm, g_ref), (x_hbm, x_ref)]
    for at in range(0, rows, TALL):
        lines = pl.ds(at, TALL)
        pairs.append((e_hbm.at[0, lines], e_ref.at[lines]))
    copies = [
        pltpu.make_async_copy(source, target, here.at[i])
        for i, (source, target) in enumerate(pairs)
    ]
    for copy in copies:
        copy.start()
    copies[0].wait()
    copies[1].wait()
    through = stacked(times_q(g_ref[...], q_ref))
    copies[2].wait()
    left = folded(mxu(through, x_ref[...], NN))
    for i, at in enumerate(range(0, rows, TALL)):
        lines = slice(at, at + TALL)
        copies[3 + i].wait()
        part = (times_q(e_ref[lines], q_ref) + left[:, lines]) * (1.0 / REPLICAS)
        for j in range(TALL // LANES):
            block = part[:, j * LANES : (j + 1) * LANES]
            part_ref[at // LANES + j] = block


def first_left(inputs, out_grads, error, q_init):
    rows = inputs.shape[1]
    operands = (inputs, out_grads, error, q_init.T)
    held = [pltpu.VMEM(a.shape[-2:], bf16) for a in operands]
    return call(
        first_left_kernel,
        shape((rows // LANES, R, LANES)),
        in_specs=[pl.BlockSpec(memory_space=pltpu.HBM)] * 4,
        out_specs=pl.BlockSpec(memory_space=pltpu.VMEM),
        scratch_shapes=held + [pltpu.SemaphoreType.DMA((3 + rows // TALL,))],
    )(*(streamed(a) for a in operands))


def merge_kernel(core_ref, x_ref, g_ref, e_ref, mine_ref, other_ref):
    merged = mxu(x_ref[...], g_ref[...], TN) + e_ref[0].astype(f32)
    half = merged.shape[1] // 2

    @pl.when(core_ref[0] == 0)
    def _():
        mine_ref[...] = merged[:, :half]
        other_ref[...] = merged[:, half:]

    @pl.when(core_ref[0] != 0)
    def _():
        mine_ref[...] = merged[:, half:]
        other_ref[...] = merged[:, :half]


def merge(core, inputs, out_grads, error):
    tokens, rows = inputs.shape
    cols = out_grads.shape[1]
    half = pl.BlockSpec((TALL, cols // 2), lambda i, c: (i, 0))
    spec = pltpu.PrefetchScalarGridSpec(
        num_scalar_prefetch=1,
        grid=(rows // TALL,),
        in_specs=[
            pl.BlockSpec((tokens, TALL), lambda i, c: (0, i)),
            pl.BlockSpec((tokens, cols), lambda i, c: (0, 0)),
            pl.BlockSpec((1, TALL, cols), lambda i, c: (0, i, 0)),
        ],
        out_specs=[half, half],
    )
    outs = (pltpu.HBM((rows, cols // 2), f32), pltpu.HBM((rows, cols // 2), f32))
    cost = pl.CostEstimate(
        flops=2 * tokens * rows * cols, bytes_accessed=12 * rows * cols, transcendentals=0
    )
    return call(merge_kernel, outs, grid_spec=spec, cost_estimate=cost)(
        core, *(streamed(a) for a in (inputs, out_grads, error))
    )


def spread_kernel(x_ref, o_ref):
    total = jnp.sum(x_ref[...], axis=0)
    o_ref[...] = jnp.broadcast_to(total[None], o_ref.shape)


def sent(blocks, axes):
    return lax.all_to_all(blocks, axes, 0, 0, tiled=True)


def spread(arrived, count):
    again = shape((count, *arrived.shape[1:]))
    return call(spread_kernel, again)(arrived)


def packed_kernel(count, x_ref, o_ref):
    lines = x_ref.shape[0] // count
    total = x_ref[:lines]
    for i in range(1, count):
        total = total + x_ref[i * lines : (i + 1) * lines]
    for i in range(count):
        o_ref[i * lines : (i + 1) * lines] = total


def all_sum(parts, axes):
    size = lax.axis_size(axes)
    rows = (size, 1, parts.size // size)
    arrived = sent(parts.reshape(rows), axes).reshape(parts.shape)
    kernel = functools.partial(packed_kernel, size)
    again = call(kernel, shape(parts.shape))(arrived)
    return sent(again.reshape(rows), axes).reshape(parts.shape)


def ring_sum(parts, outer, inner):
    count = lax.axis_size(outer)
    lines = parts.shape[0] * parts.shape[1] // count
    arrived = sent(parts.reshape(count, lines, LANES), outer)
    arrived = sent(spread(arrived, lax.axis_size(inner)), inner)
    return sent(spread(arrived, count), outer).reshape(parts.shape)


def side_by_side(ref, count):
    return jnp.concatenate([ref[i] for i in range(count)], axis=1)


def right_lines(cols):
    return cols // LANES * R + GRAM_LINES, LANES


def right_of(ref):
    blocks = ref.shape[0] // R
    return jnp.concatenate([ref[i * R : (i + 1) * R] for i in range(blocks)], axis=1)


def gram_of(ref):
    lines = ref[...]
    return jnp.concatenate([lines[:, :R], lines[:, R:]], axis=0)


def store_right(left, high, low, out_ref):
    blocks = high.shape[1] // LANES
    left_pieces = stacked(left)
    right = folded(mxu(left_pieces, high, NN) + mxu(left_pieces, low, NN))
    right = right * (1.0 / REPLICAS)
    for i in range(blocks):
        out_ref[i * R : (i + 1) * R] = right[:, i * LANES : (i + 1) * LANES]
    part = gram(left) * (1.0 / GRAM_COPIES)
    out_ref[blocks * R :] = jnp.concatenate(
        [part[:GRAM_LINES], part[GRAM_LINES:]], axis=1
    )


def halve_kernel(mine_ref, came_ref, high_ref, low_ref):
    high_ref[...], low_ref[...] = pieces(mine_ref[...] + came_ref[...])


def halve(mine, came):
    outs = (shape(mine.shape, bf16), shape(mine.shape, bf16))
    cost = pl.CostEstimate(
        flops=3 * mine.size, bytes_accessed=12 * mine.size, transcendentals=0
    )
    block = pl.BlockSpec((TALL, mine.shape[1]), lambda i: (i, 0))
    return call(
        halve_kernel,
        outs,
        grid=(mine.shape[0] // TALL,),
        in_specs=[block, block],
        out_specs=[block, block],
        cost_estimate=cost,
    )(streamed(mine), streamed(came))


def first_right_kernel(left_ref, high_ref, low_ref, out_ref):
    left = side_by_side(left_ref, left_ref.shape[0])
    store_right(left, high_ref[...], low_ref[...], out_ref)


def first_right(left, high, low):
    outs = shape(right_lines(high.shape[1]))
    return call(first_right_kernel, outs)(left, high, low)


def left_kernel(right_ref, high_ref, low_ref, out_ref):
    right = stacked(right_of(right_ref))
    left = mxu(right, high_ref[...], NT) + mxu(right, low_ref[...], NT)
    left = folded(left) * (1.0 / REPLICAS)
    for i in range(out_ref.shape[0]):
        out_ref[i] = left[:, i * LANES : (i + 1) * LANES]


def left_part(right, high, low):
    outs = shape((high.shape[0] // LANES, R, LANES))
    return call(left_kernel, outs)(right, high, low)


def second_right_kernel(
    inverse_ref, raw_ref, high_ref, low_ref, out_ref, left_ref
):
    raw = side_by_side(raw_ref, raw_ref.shape[0])
    left = exact(inverse_ref[...], raw)
    left_ref[...] = left
    store_right(left, high_ref[...], low_ref[...], out_ref)


def second_right(inverse, raw, high, low):
    rows, cols = high.shape
    outs = (shape(right_lines(cols)), shape((R, rows)))
    return call(second_right_kernel, outs)(inverse, raw, high, low)


def lower_inverse(gram):
    row = lax.broadcasted_iota(jnp.int32, (R, R), 0)
    column = lax.broadcasted_iota(jnp.int32, (R, R), 1)
    work = jnp.concatenate([gram, (row == column).astype(f32)], axis=1)
    bands = [work[8 * i : 8 * i + 8] for i in range(R // 8)]
    below = lax.broadcasted_iota(jnp.int32, (8, LANES), 0)
    scales = []
    for p in range(R // 8):
        live = range(p, R // 8)
        spread = {
            i: [
                jnp.broadcast_to(bands[i][:, 8 * p + c : 8 * p + c + 1], (8, LANES))
                for c in range(8)
            ]
            for i in live
        }
        for k in range(8):
            pivot_row = bands[p][k : k + 1]
            pivots = [spread[p][c][k : k + 1] for c in range(8)]
            scales.append(lax.rsqrt(pivots[k]))
            inverse = 1.0 / pivots[k]
            for i in live:
                factor = spread[i][k] * inverse
                if i == p:
                    factor = jnp.where(below > k, factor, 0.0)
                for c in range(k + 1, 8):
                    spread[i][c] = spread[i][c] - factor * pivots[c]
                bands[i] = bands[i] - factor * pivot_row
    out = []
    for i in range(R // 8):
        scale = jnp.concatenate(scales[8 * i : 8 * i + 8], axis=0)
        out.append(bands[i][:, R:] * scale[:, R:])
    return jnp.concatenate(out, axis=0)


def inverse_kernel(right_ref, out_ref):
    out_ref[...] = lower_inverse(gram_of(right_ref))


def last_block(right):
    last = right.shape[0] // GRAM_LINES - 1
    return pl.BlockSpec((GRAM_LINES, LANES), lambda i: (last, 0))


def inverse_of(right):
    return call(
        inverse_kernel,
        shape((R, R)),
        grid=(1,),
        in_specs=[last_block(right)],
        out_specs=pl.BlockSpec((R, R), lambda i: (0, 0)),
    )(right)


def basis_kernel(
    right_ref, left_ref, x_ref, g_ref, e_ref, inverse_ref, basis_ref, factor_ref, merged_ref
):
    merged_ref[...] = mxu(x_ref[...].T, g_ref[...], NN) + e_ref[0].astype(f32)
    inverse = lower_inverse(gram_of(right_ref))
    inverse_ref[...] = inverse
    basis = exact(inverse, left_ref[...])
    factor_ref[...] = (basis * math.sqrt(D)).astype(bf16)
    basis_ref[...] = across(basis.T)


def basis_of(right, left, inputs, out_grads, error):
    rows = left.shape[1]
    merged = (rows, out_grads.shape[1])
    return call(
        basis_kernel,
        (
            shape((R, R)),
            shape((rows, 4 * R), bf16),
            shape((R, rows), bf16),
            shape(merged),
        ),
        in_specs=[last_block(right)] + [pl.BlockSpec(memory_space=pltpu.VMEM)] * 4,
        out_specs=[pl.BlockSpec(memory_space=pltpu.VMEM)] * 4,
        grid=(1,),
    )(right, left, inputs, out_grads, error)


def error_kernel(
    core_ref, inverse_ref, own_ref, came_ref, basis_ref, p_ref, merged_ref,
    new_ref, p_out_ref, q_out_ref, held_ref, done_ref, q_ref, sent_sem,
):
    count, _, step = done_ref.shape
    copies = []

    def leave(source, target):
        copies.append(pltpu.make_async_copy(source, target, sent_sem.at[len(copies)]))
        copies[-1].start()

    leave(p_ref, p_out_ref)
    width = merged_ref.shape[1] // 2
    inverse = across(inverse_ref[...])
    for half, raw_ref in enumerate((own_ref, came_ref)):
        start = lax.rem(core_ref[0] + half, 2) * width
        columns = pl.ds(pl.multiple_of(start, LANES), width)
        raw = right_of(raw_ref)
        right = mxu(inverse, down(raw), NN)
        q_ref[:, columns] = right.astype(bf16)
        held_ref[:, columns] = down(right)
    leave(q_ref, q_out_ref)
    for i in range(count):
        columns = pl.ds(i * step, step)
        approximation = mxu(basis_ref[...], held_ref[:, columns], NN)
        done_ref[i] = (merged_ref[:, columns] - approximation).astype(bf16)
        leave(done_ref.at[i], new_ref.at[0, :, columns])
    for copy in copies:
        copy.wait()


def final(core, inverse, own, came, basis, p_factor, merged):
    rows, cols = merged.shape
    step = 2 * LANES
    count = cols // step
    vmem = pl.BlockSpec(memory_space=pltpu.VMEM)
    outs = (shape((1, rows, cols), bf16), shape((R, rows), bf16), shape((R, cols), bf16))
    return call(
        error_kernel,
        outs,
        in_specs=[pl.BlockSpec(memory_space=pltpu.SMEM)] + [vmem] * 6,
        out_specs=[pl.BlockSpec(memory_space=pltpu.HBM)] * 3,
        scratch_shapes=[
            pltpu.VMEM((4 * R, cols), bf16),
            pltpu.VMEM((count, rows, step), bf16),
            pltpu.VMEM((R, cols), bf16),
            pltpu.SemaphoreType.DMA((count + 2,)),
        ],
    )(core, inverse, own, came, basis, p_factor, merged)


def shards(inputs, out_grads, error, q_init):
    core = lax.axis_index("core").reshape(1)
    swap = [(0, 1), (1, 0)]
    part = first_left(inputs, out_grads, error, q_init)
    mine, other = merge(core, inputs, out_grads, error)
    came = lax.ppermute(other, "core", swap)
    left = ring_sum(part, XC, "z")
    high, low = halve(mine, came)
    right = all_sum(first_right(left, high, low), XY)
    inverse = inverse_of(right)
    raw = ring_sum(left_part(right, high, low), XC, "z")
    part, left = second_right(inverse, raw, high, low)
    own = all_sum(part, XY)
    came = lax.ppermute(own, "core", swap)
    inverse, basis, p_factor, merged = basis_of(own, left, inputs, out_grads, error)
    new_error, p_factor, q_factor = final(
        core, inverse, own, came, basis, p_factor, merged
    )
    return new_error, p_factor.T, q_factor.T


def solution(mesh):
    rep, fsdp, tp = mesh.devices.shape
    fine = Mesh(mesh.devices.reshape(rep // 2, 2, fsdp, tp), ("x", "core", "z", "y"))
    both = ("x", "core")
    in_specs = (P(both, "y"), P(both, "z"), P(both, "y", "z"), P("z", None))
    out_specs = (P(both, "y", "z"), P("y", None), P("z", None))
    return jax.shard_map(
        shards, mesh=fine, in_specs=in_specs, out_specs=out_specs, check_vma=False
    )
```
